32 devices in a mesh: parts: 2 (over y), tm: 4 (over x, core), span: 4 (over z).
Axes of the slice: x: 2, y: 2, z: 4, core: 2. Of those that a mesh axis runs over, the one named last changes fastest.
Arguments:
- start_state: float32 [2, 512, 1024], P(None, ('parts', 'span')), parts along dimension 1, may hold values from -4 to 4
- stiff_class: int32 [2048], P('parts'), parts along dimension 0, may hold values from 0 to 5
- class_stiffness: float32 [6], replicated, may hold values from 0.5 to 2
- axle_rows: int32 [64, 8], P(('parts', 'tm')), parts along dimension 0, may hold values from 0 to 255
- axle_cols: int32 [64, 8], P(('parts', 'tm')), parts along dimension 0, may hold values from 0 to 1023
- axle_class: int32 [64, 8], P(('parts', 'tm')), parts along dimension 0, may hold values from 0 to 4
- load_table: float32 [5], replicated, may hold values from 2 to 20
Outputs:
- end_states: float32 [4, 2, 512, 1024], P('tm', None, ('parts', 'span')), parts along dimension 2
The draws below stay inside these ranges and needn't reach their ends.
There are 2 independent parts, one for each index of `parts`. The reference program is written for one: setup_inputs(seed, part) draws one part's arguments, and reference() takes and returns one part's arrays. A program takes and returns all parts, laid end to end along the dimension named above; an argument that names none is the same for every part. Nothing has to cross between parts.
All inputs are finite; a program needn't handle non-finite values.
Results may differ from the reference program's by a relative error of at most 0.00027.
Values sent between devices are 32-bit elements; how exact they have to be, the bound alone decides.
No kernel may reach another device: no remote copies, remote signals or barrier semaphores. Data moves between devices by JAX's collectives and lax.ppermute only.
A program may use at most 128 MiB of HBM per device.

```python
import math
import jax
import jax.numpy as jnp

W = 1024
FSTEPS = 8
AXLES = 8
NCLS = 6
NLOAD = 5
SLICES = 4
L = 256
LC = 64
WC = 256
STEPS = 32


def touch_ends(values, rng, smallest, largest):
    place = [jax.random.randint(jax.random.fold_in(rng, axis), (), 0, length) for axis, length in enumerate(values.shape)]
    longest = values.shape.index(max(values.shape))
    beside = place[:longest] + [(place[longest] + 1) % values.shape[longest]] + place[longest + 1:]
    return values.at[tuple(place)].set(smallest).at[tuple(beside)].set(largest)


def block_levels(key, extent, split, least, high):
    factor_of = 1.0
    for axis_at, shards_of in split:
        steps = jax.random.uniform(jax.random.fold_in(jax.random.fold_in(key, 6), axis_at), (shards_of,), jnp.float32, least / len(split), high / len(split))
        factor_of = factor_of * jnp.repeat(jnp.exp(steps), extent[axis_at] // shards_of).reshape((-1,) + (1,) * (len(extent) - 1 - axis_at))
    return factor_of


def noise(stream_key, dims, scale, most, shards=(), dtype=jnp.bfloat16):
    factor_of = block_levels(stream_key, dims, shards, -0.22, 0.18) if shards else 1.0
    values = jax.random.normal(stream_key, dims, jnp.float32) * scale * factor_of
    return jnp.minimum(jnp.maximum(values, -most), most).astype(dtype)


def setup_inputs(seed: int = 0, part: int = 0) -> dict:
    streams_of = jax.random.split(jax.random.key(seed), 8)
    part_keys = jax.random.split(jax.random.fold_in(streams_of[7], part), 8)
    start_state = noise(part_keys[0], (2, L, W), 0.5, 4.0, ((1, 4),), jnp.float32)
    stiff_class = touch_ends(jax.random.randint(part_keys[1], (W,), 0, NCLS), jax.random.fold_in(part_keys[1], 1), 0, NCLS - 1).astype(jnp.int32)
    class_stiffness = jnp.clip(jnp.exp(jax.random.uniform(streams_of[2], (NCLS,), jnp.float32, math.log(0.5), math.log(2.0))), 0.5, 2.0)
    axle_rows = touch_ends(jax.random.randint(part_keys[3], (STEPS, AXLES), 0, L), jax.random.fold_in(part_keys[3], 1), 0, L - 1).astype(jnp.int32)
    axle_cols = touch_ends(jax.random.randint(part_keys[4], (STEPS, AXLES), 0, W), jax.random.fold_in(part_keys[4], 1), 0, W - 1).astype(jnp.int32)
    axle_class = touch_ends(jax.random.randint(part_keys[5], (STEPS, AXLES), 0, NLOAD), jax.random.fold_in(part_keys[5], 1), 0, NLOAD - 1).astype(jnp.int32)
    load_table = jnp.clip(jnp.exp(jax.random.uniform(streams_of[6], (NLOAD,), jnp.float32, math.log(2.0), math.log(20.0))), 2.0, 20.0)
    return dict(start_state=start_state, stiff_class=stiff_class, class_stiffness=class_stiffness, axle_rows=axle_rows, axle_cols=axle_cols, axle_class=axle_class, load_table=load_table)


TIME_STEP = 0.2
DAMPING = 0.05
TWIST = 0.5
CROSS_STIFF = 1.0
COARSE_SPACING = 256.0


def stiffness_term(padded, column_stiff):
    widened = jnp.pad(padded, ((0, 0), (2, 2)))
    along_rows = widened[2:] - 2.0 * widened[1:-1] + widened[:-2]
    along_four = along_rows[2:] - 2.0 * along_rows[1:-1] + along_rows[:-2]
    across = widened[:, 2:] - 2.0 * widened[:, 1:-1] + widened[:, :-2]
    across_four = across[:, 2:] - 2.0 * across[:, 1:-1] + across[:, :-2]
    mixed_term = across[2:] - 2.0 * across[1:-1] + across[:-2]
    return column_stiff * along_four[:, 2:-2] + (2.0 * TWIST) * mixed_term[1:-1, 1:-1] + CROSS_STIFF * across_four[2:-2]


def advance(padded, deflect, velocity, column_stiff, loading, spacing, time_step):
    velocity = (1.0 - time_step * DAMPING) * velocity + time_step * (loading - stiffness_term(padded, column_stiff) / spacing)
    return deflect + time_step * velocity, velocity


def restrict(fine_field):
    leading = fine_field.shape[:-2]
    row_count = fine_field.shape[-2]
    col_count = fine_field.shape[-1]
    return jnp.mean(fine_field.reshape(leading + (row_count // 4, 4, col_count // 4, 4)), axis=(-3, -1))


def prolong(coarse):
    return jnp.repeat(jnp.repeat(coarse, 4, axis=-2), 4, axis=-1)


def reference(start_state, stiff_class, class_stiffness, axle_rows, axle_cols, axle_class, load_table):
    column_stiff = class_stiffness[stiff_class]
    coarse_stiff = jnp.mean(column_stiff.reshape(WC, 4), axis=-1)
    weights = load_table[axle_class]

    def fine_load(moment):
        return jnp.zeros((L, W), jnp.float32).at[axle_rows[moment], axle_cols[moment]].add(weights[moment])

    coarse_loads = []
    for slice_number in range(SLICES):
        total = jnp.zeros((LC, WC), jnp.float32)
        for substep in range(FSTEPS):
            total = total + restrict(fine_load(slice_number * FSTEPS + substep))
        coarse_loads.append(total / FSTEPS)

    def coarse_step(fields, slice_number):
        deflect, velocity = advance(jnp.pad(fields[0], ((2, 2), (0, 0))), fields[0], fields[1], coarse_stiff,
                                    coarse_loads[slice_number], COARSE_SPACING, TIME_STEP * FSTEPS)
        return jnp.stack([deflect, velocity])

    def fine_sweep(fields, slice_number):
        deflect, velocity = fields[0], fields[1]
        for substep in range(FSTEPS):
            loading = fine_load(slice_number * FSTEPS + substep)
            deflect, velocity = advance(jnp.pad(deflect, ((2, 2), (0, 0))), deflect, velocity, column_stiff,
                                        loading, 1.0, TIME_STEP)
        return jnp.stack([deflect, velocity])

    anchor = restrict(start_state)
    first_chain = [anchor]
    for slice_number in range(SLICES - 1):
        first_chain.append(coarse_step(first_chain[-1], slice_number))
    first_starts = [start_state] + [prolong(first_chain[k]) for k in range(1, SLICES)]
    first_sweeps = [fine_sweep(first_starts[k], k) for k in range(SLICES)]

    second_chain = [anchor]
    for slice_number in range(SLICES - 1):
        old_value = coarse_step(first_chain[slice_number], slice_number)
        second_chain.append(coarse_step(second_chain[-1], slice_number)
                            + (restrict(first_sweeps[slice_number]) - old_value))
    second_starts = [start_state] + [first_sweeps[k - 1] + prolong(second_chain[k] - restrict(first_sweeps[k - 1]))
                                     for k in range(1, SLICES)]
    second_sweeps = [fine_sweep(second_starts[k], k) for k in range(SLICES)]

    ends = []
    current = anchor
    for slice_number in range(SLICES):
        old_value = coarse_step(second_chain[slice_number], slice_number)
        following = coarse_step(current, slice_number) + (restrict(second_sweeps[slice_number]) - old_value)
        ends.append(second_sweeps[slice_number] + prolong(following - restrict(second_sweeps[slice_number])))
        current = following
    return jnp.stack(ends)
```

```python
import jax
import jax.numpy as jnp
from jax import lax
from jax.experimental import pallas as pl
from jax.experimental.pallas import tpu as pltpu
from jax.sharding import PartitionSpec as P

TIME_STEP = 0.2
DAMPING = 0.05
TWIST = 0.5
CROSS_STIFF = 1.0
COARSE_SPACING = 256.0


def extended(cells, sides, width):
    for axis, dim in sides:
        count = lax.axis_size(axis)
        ends = count - 1
        head = lax.slice_in_dim(cells, 0, width, axis=dim)
        tail = lax.slice_in_dim(cells, cells.shape[dim] - width, cells.shape[dim], axis=dim)
        cells = jnp.concatenate(
            [
                lax.ppermute(tail, axis, [(i, (i + 1) % count) for i in range(ends)]),
                cells,
                lax.ppermute(head, axis, [((i + 1) % count, i) for i in range(ends)]),
            ],
            axis=dim,
        )
    return cells


def shifted(value, axis, steps):
    count = lax.axis_size(axis)
    leading, last = (max(0, -steps), min(count, count - steps))
    return lax.ppermute(value, axis, [(source, source + steps) for source in range(leading, last)])


def stiffness_term(padded, column_stiff):
    widened = jnp.pad(padded, ((0, 0), (2, 2)))
    along_rows = widened[2:] - 2.0 * widened[1:-1] + widened[:-2]
    along_four = along_rows[2:] - 2.0 * along_rows[1:-1] + along_rows[:-2]
    across = widened[:, 2:] - 2.0 * widened[:, 1:-1] + widened[:, :-2]
    across_four = across[:, 2:] - 2.0 * across[:, 1:-1] + across[:, :-2]
    mixed_term = across[2:] - 2.0 * across[1:-1] + across[:-2]
    return (
        column_stiff * along_four[:, 2:-2]
        + 2.0 * TWIST * mixed_term[1:-1, 1:-1]
        + CROSS_STIFF * across_four[2:-2]
    )


def advance(padded, deflect, velocity, column_stiff, loading, spacing, time_step):
    velocity = (1.0 - time_step * DAMPING) * velocity + time_step * (
        loading - stiffness_term(padded, column_stiff) / spacing
    )
    return (deflect + time_step * velocity, velocity)


def restrict(fine_field):
    leading = fine_field.shape[:-2]
    row_count = fine_field.shape[-2]
    col_count = fine_field.shape[-1]
    return jnp.mean(
        fine_field.reshape(leading + (row_count // 4, 4, col_count // 4, 4)), axis=(-3, -1)
    )


def prolong(coarse):
    return jnp.repeat(jnp.repeat(coarse, 4, axis=-2), 4, axis=-1)


def table_lookup(indices, table):
    entries = table.shape[0]
    matches = indices[..., None] == lax.iota(jnp.int32, entries)
    return jnp.sum(jnp.where(matches, table, 0.0), axis=-1)


def point_loads(axle_row, axle_col, weights, first_row, row_total, col_total):
    row_hot = jnp.where(
        axle_row[:, None] - first_row == lax.iota(jnp.int32, row_total)[None, :],
        weights[:, None],
        0.0,
    )
    col_hot = jnp.where(axle_col[:, None] == lax.iota(jnp.int32, col_total)[None, :], 1.0, 0.0)
    return jnp.einsum(
        "ar,ac->rc",
        row_hot,
        col_hot,
        precision=lax.Precision.HIGHEST,
        preferred_element_type=jnp.float32,
    )


def coarse_loading(step_rows, step_cols, weights, first_row, coarse_count, coarse_cols):
    step_total = step_rows.shape[0]
    scaled = weights.reshape(-1) / (16.0 * step_total)
    return point_loads(
        step_rows.reshape(-1) // 4,
        step_cols.reshape(-1) // 4,
        scaled,
        first_row,
        coarse_count,
        coarse_cols,
    )


def on_device(
    start_state, stiff_class, class_stiffness, axle_rows, axle_cols, axle_class, load_table
):
    slice_count = lax.axis_size("tm")
    tile_index = lax.axis_index("span")
    slice_index = lax.axis_index("tm")
    tile_rows = start_state.shape[1]
    width = start_state.shape[2]
    coarse_cols = width // 4
    fine_steps = axle_rows.shape[0]
    coarse_first = tile_index * (tile_rows // 4)
    coarse_count = tile_rows // 4
    column_stiff = table_lookup(stiff_class, class_stiffness)
    coarse_stiff = jnp.mean(column_stiff.reshape(coarse_cols, 4), axis=-1)
    weights = table_lookup(axle_class, load_table)
    own_loading = coarse_loading(
        axle_rows, axle_cols, weights, coarse_first, coarse_count, coarse_cols
    )
    coarse_tau = TIME_STEP * fine_steps

    def coarse_step(fields, loading):
        padded = extended(fields[0], (("span", 0),), 2)
        deflect, velocity = advance(
            padded, fields[0], fields[1], coarse_stiff, loading, COARSE_SPACING, coarse_tau
        )
        return jnp.stack([deflect, velocity])

    def relay(anchor, correction):

        def one_round(round_index, current):
            advanced = coarse_step(current, own_loading)
            if correction is not None:
                advanced = advanced + correction
            moved = shifted(advanced, "tm", 1)
            return jnp.where(slice_index == 0, anchor, moved)

        return lax.fori_loop(0, slice_count - 1, one_round, anchor)

    def fine_sweep(fields):
        deflect, velocity = (fields[0], fields[1])
        first_row = tile_index * tile_rows
        for substep in range(fine_steps):
            padded = extended(deflect, (("span", 0),), 2)
            loading = point_loads(
                axle_rows[substep],
                axle_cols[substep],
                weights[substep],
                first_row,
                tile_rows,
                width,
            )
            deflect, velocity = advance(
                padded, deflect, velocity, column_stiff, loading, 1.0, TIME_STEP
            )
        return jnp.stack([deflect, velocity])

    anchor = restrict(start_state)
    first_chain = relay(anchor, None)
    first_old = coarse_step(first_chain, own_loading)
    start_zero = jnp.where(slice_index == 0, start_state, prolong(first_chain))
    sweep_zero = fine_sweep(start_zero)
    second_chain = relay(anchor, restrict(sweep_zero) - first_old)
    second_old = coarse_step(second_chain, own_loading)
    prior = shifted(sweep_zero, "tm", 1)
    start_one = jnp.where(
        slice_index == 0, start_state, prior + prolong(second_chain - restrict(prior))
    )
    sweep_one = fine_sweep(start_one)
    third_correction = restrict(sweep_one) - second_old
    third_chain = relay(anchor, third_correction)
    following = coarse_step(third_chain, own_loading) + third_correction
    end_state = sweep_one + prolong(following - restrict(sweep_one))
    return end_state[None]


SLICES = 4
LANES = 128
GROUPS = 8
MARGIN = 8
BLOCK = 32
REACH = 48
CREACH = REACH // 4
RATIO = TIME_STEP * TIME_STEP


def lane_index(rows):
    return lax.broadcasted_iota(jnp.int32, (rows, LANES), 1)


def from_left(x):
    lane = lane_index(x.shape[0])
    source = jnp.where(lane < 8, (lane + 119) % LANES, lane - 8)
    moved = jnp.take_along_axis(x, source, axis=1, mode="promise_in_bounds")
    return jnp.where(lane == 0, 0.0, moved)


def from_right(x):
    lane = lane_index(x.shape[0])
    source = jnp.where(lane >= 120, (lane + 9) % LANES, lane + 8)
    moved = jnp.take_along_axis(x, source, axis=1, mode="promise_in_bounds")
    return jnp.where(lane == LANES - 1, 0.0, moved)


def interleave(pieces):
    pieces = list(pieces)
    lane = lane_index(pieces[0].shape[0])
    for dist in (1, 2, 4):
        keep = (lane & dist) == 0
        for low in range(GROUPS):
            if low & dist:
                continue
            high = low + dist
            first, second = pieces[low], pieces[high]
            pieces[low] = jnp.where(keep, first, pltpu.roll(second, dist, 1))
            pieces[high] = jnp.where(keep, pltpu.roll(first, LANES - dist, 1), second)
    return pieces


def tall(row_vreg, rows):
    return jnp.concatenate([row_vreg] * (rows // 8), axis=0)


class Plan:
    def __init__(self, tile_rows, span, steps, axles):
        self.tile = tile_rows
        self.rows = tile_rows + 2 * REACH
        self.buf = self.rows + 2 * MARGIN
        self.crows = self.rows // 4
        self.cbuf = self.crows + 2 * MARGIN
        self.span = span
        self.steps = steps
        self.axles = axles
        self.coarse_tau = TIME_STEP * steps

    def stiffness(self, classes_ref, table_ref, coef, ccoef):
        entries = table_ref.shape[0]
        pieces = []
        for q in range(GROUPS):
            cls = jnp.broadcast_to(classes_ref[:, q * LANES : (q + 1) * LANES], (8, LANES))
            value = jnp.zeros((8, LANES), jnp.float32)
            for entry in range(entries):
                value = jnp.where(cls == entry, table_ref[entry], value)
            pieces.append(value)
        stiff = interleave(pieces)
        for a in range(GROUPS):
            s = stiff[a]
            coef[0, a] = (2.0 - TIME_STEP * DAMPING) - RATIO * (6.0 * s + 10.0)
            coef[1, a] = RATIO * (4.0 * s + 2.0)
            coef[2, a] = -RATIO * s
        for g in range(2):
            ccoef[g] = 0.25 * (stiff[4 * g] + stiff[4 * g + 1] + stiff[4 * g + 2] + stiff[4 * g + 3])

    def clear_outside(self, ref, tile_index):
        @pl.when(tile_index == 0)
        def _():
            for a in range(GROUPS):
                ref[a, pl.ds(MARGIN + REACH - 8, 8), :] = jnp.zeros((8, LANES), jnp.float32)

        @pl.when(tile_index == self.span - 1)
        def _():
            for a in range(GROUPS):
                ref[a, pl.ds(MARGIN + REACH + self.tile, 8), :] = jnp.zeros((8, LANES), jnp.float32)

    def block(self, src, dst, coef, r0):
        def at(a, offset):
            return src[a, pl.ds(r0 + offset, BLOCK), :]

        w, s1, t = {}, {}, {}

        def make(a):
            w[a] = at(a, 0)
            s1[a] = at(a, -1) + at(a, 1)
            t[a] = s1[a] - 6.0 * w[a]

        for a in (6, 7, 0, 1):
            make(a)
        w[-2], w[-1], t[-1] = from_left(w[6]), from_left(w[7]), from_left(t[7])
        w[8], w[9], t[8] = from_right(w[0]), from_right(w[1]), from_right(t[0])
        for a in range(GROUPS):
            if a + 2 not in w:
                make(a + 2)
            s2 = at(a, -2) + at(a, 2)
            across = (t[a - 1] + t[a + 1]) + (w[a - 2] + w[a + 2])
            along = tall(coef[2, a], BLOCK) * s2 + tall(coef[1, a], BLOCK) * s1[a]
            along = along + tall(coef[0, a], BLOCK) * w[a]
            old = dst[a, pl.ds(r0, BLOCK), :]
            dst[a, pl.ds(r0, BLOCK), :] = along - RATIO * across - (1.0 - TIME_STEP * DAMPING) * old

    def axle(self, ax, loads, number, step, i):
        per = self.steps * self.axles
        base = number * (3 * per) + step * self.axles + i
        return ax[base], ax[base + per], loads[ax[base + 2 * per]]

    def sweep(self, cur, prev, coef, ax, loads, number, first, blocks, tile_index):
        origin = tile_index * self.tile - REACH

        def advance_once(src, dst, step):
            def one(j, carry):
                self.block(src, dst, coef, pl.multiple_of(MARGIN + first + j * BLOCK, 8))
                return carry

            lax.fori_loop(0, blocks, one, 0)
            lane = lane_index(1)
            for i in range(self.axles):
                row, col, weight = self.axle(ax, loads, number, step, i)
                local = row - origin
                inside = jnp.logical_and(local >= 0, local < self.rows)
                force = jnp.where(inside, RATIO * weight, 0.0)
                place = jnp.where(inside, local, 0) + MARGIN
                where = ((col >> 3) & 15) * 8 + (col >> 7)
                group = col & 7
                here = dst[group, pl.ds(place, 1), :]
                dst[group, pl.ds(place, 1), :] = here + jnp.where(lane == where, force, 0.0)
            self.clear_outside(dst, tile_index)

        def two(half, carry):
            advance_once(cur, prev, 2 * half)
            advance_once(prev, cur, 2 * half + 1)
            return carry

        lax.fori_loop(0, self.steps // 2, two, 0)

    def inside(self, tile_index):
        row = lax.broadcasted_iota(jnp.int32, (self.crows, LANES), 0)
        row = row + (tile_index * (self.tile // 4) - CREACH)
        return jnp.logical_and(row >= 0, row < self.span * (self.tile // 4))

    def restricted(self, cur, prev, tile_index):
        keep = self.inside(tile_index)
        fields = []
        for ref in (cur, prev):
            halves = []
            for g in range(2):
                total = None
                for a in range(4 * g, 4 * g + 4):
                    for j in range(4):
                        piece = ref[a, pl.ds(MARGIN + j, self.crows, stride=4), :]
                        total = piece if total is None else total + piece
                halves.append(jnp.where(keep, total * 0.0625, 0.0))
            fields.append(halves)
        now, before = fields
        return now, [now[g] - before[g] for g in range(2)]

    def add_prolonged(self, cur, prev, field, fresh):
        now, change = field
        for g in range(2):
            before = now[g] - change[g]
            for a in range(4 * g, 4 * g + 4):
                for j in range(4):
                    place = pl.ds(MARGIN + j, self.crows, stride=4)
                    if fresh:
                        cur[a, place, :] = now[g]
                        prev[a, place, :] = before
                    else:
                        cur[a, place, :] = cur[a, place, :] + now[g]
                        prev[a, place, :] = prev[a, place, :] + before

    def coarse_loads(self, cload, ax, loads, number, tile_index):
        origin = tile_index * (self.tile // 4) - CREACH
        for g in range(2):
            cload[g] = jnp.zeros((self.cbuf, LANES), jnp.float32)
        lane = lane_index(1)
        scale = TIME_STEP * self.coarse_tau / (16.0 * self.steps)

        def one_step(step, carry):
            for i in range(self.axles):
                row, col, weight = self.axle(ax, loads, number, step, i)
                local = (row >> 2) - origin
                inside = jnp.logical_and(local >= 0, local < self.crows)
                force = jnp.where(inside, scale * weight, 0.0)
                place = jnp.where(inside, local, 0) + MARGIN
                where = ((col >> 3) & 15) * 8 + (col >> 7)
                group = (col >> 2) & 1
                here = cload[group, pl.ds(place, 1), :]
                cload[group, pl.ds(place, 1), :] = here + jnp.where(lane == where, force, 0.0)
            return carry

        lax.fori_loop(0, self.steps, one_step, 0)

    def coarse(self, field, cwork, ccoef, tile_index, cload=None):
        now, change = field
        rows = self.crows
        for g in range(2):
            cwork[g, pl.ds(MARGIN, rows), :] = now[g]

        def at(g, offset):
            return cwork[g, pl.ds(MARGIN + offset, rows), :]

        keep = self.inside(tile_index)
        w = now
        s1 = [at(g, -1) + at(g, 1) for g in range(2)]
        s2 = [at(g, -2) + at(g, 2) for g in range(2)]
        t = [s1[g] - 6.0 * w[g] for g in range(2)]
        left, right = [from_left(t[1]), t[0]], [t[1], from_right(t[0])]
        kappa = TIME_STEP * self.coarse_tau / COARSE_SPACING
        grown, moved = [], []
        for g in range(2):
            s = tall(ccoef[g], rows)
            across = (left[g] + right[g]) + (from_left(w[g]) + from_right(w[g]))
            stiff = across + s * s2[g] - (4.0 * s + 2.0) * s1[g] + (6.0 * s + 10.0) * w[g]
            value = (1.0 - self.coarse_tau * DAMPING) * change[g] - kappa * stiff
            if cload is not None:
                value = value + cload[g, pl.ds(MARGIN, rows), :]
            value = jnp.where(keep, value, 0.0)
            moved.append(value)
            grown.append(w[g] + (self.coarse_tau / TIME_STEP) * value)
        return grown, moved


def put(ref, slot, field):
    for f in range(2):
        for g in range(2):
            ref[slot, f, g] = field[f][g]


def get(ref, slot):
    return [[ref[slot, f, g] for g in range(2)] for f in range(2)]


def plus(x, y):
    return [[x[f][g] + y[f][g] for g in range(2)] for f in range(2)]


def minus(x, y):
    return [[x[f][g] - y[f][g] for g in range(2)] for f in range(2)]


def first_kernel(plan):
    def body(meta, ax, loads, table, classes, own, one_side, other_side, state, send, keep, coef, ccoef,
             cwork, cload, *rest):
        number, tile_index = meta[0], meta[1]
        cur, prev = state.at[0], state.at[1]
        plan.stiffness(classes, table, coef, ccoef)
        for g in range(2):
            cwork[g] = jnp.zeros((plan.cbuf, LANES), jnp.float32)
        for a in range(GROUPS):
            for f in range(2):
                state[f, a, pl.ds(0, MARGIN), :] = jnp.zeros((MARGIN, LANES), jnp.float32)
                state[f, a, pl.ds(MARGIN + plan.rows, MARGIN), :] = jnp.zeros((MARGIN, LANES), jnp.float32)

        def load_rows(ref, offset, count):
            def one(j, carry):
                r = pl.multiple_of(j * 16, 16)
                fields = []
                for f in range(2):
                    fields.append(interleave(
                        [ref[f, pl.ds(r, 16), q * LANES : (q + 1) * LANES] for q in range(GROUPS)]))
                place = pl.multiple_of(MARGIN + offset + r, 8)
                for a in range(GROUPS):
                    cur[a, pl.ds(place, 16), :] = fields[0][a]
                    prev[a, pl.ds(place, 16), :] = fields[0][a] - TIME_STEP * fields[1][a]
                return carry

            lax.fori_loop(0, count // 16, one, 0)

        even = (tile_index & 1) == 0
        load_rows(own, REACH, plan.tile)
        load_rows(one_side, jnp.where(even, REACH + plan.tile, 0), REACH)
        load_rows(other_side, jnp.where(even, 0, REACH + plan.tile), REACH)
        plan.clear_outside(cur, tile_index)
        plan.clear_outside(prev, tile_index)
        send[...] = jnp.zeros(send.shape, jnp.float32)

        def sweep(slice_number, first, blocks):
            plan.sweep(cur, prev, coef, ax, loads, slice_number, first, blocks, tile_index)

        @pl.when(number >= 2)
        def _():
            put(keep, 0, plan.restricted(cur, prev, tile_index))

        sweep(0, 0, plan.rows // BLOCK)

        @pl.when(number >= 2)
        def _():
            plan.coarse_loads(cload, ax, loads, 0, tile_index)
            chain = plan.coarse(get(keep, 0), cwork, ccoef, tile_index, cload)
            put(keep, 0, chain)
            gap = minus(plan.restricted(cur, prev, tile_index), chain)
            put(keep, 1, plan.coarse(gap, cwork, ccoef, tile_index))

        @pl.when(number == 3)
        def _():
            plan.coarse_loads(cload, ax, loads, 1, tile_index)
            put(keep, 0, plan.coarse(get(keep, 0), cwork, ccoef, tile_index, cload))

        @pl.when((number & 1) == 1)
        def _():
            sweep(1, 16, (plan.rows - 32) // BLOCK)

        @pl.when(number == 3)
        def _():
            restricted = plan.restricted(cur, prev, tile_index)
            put(send, 0, restricted)
            put(keep, 2, restricted)

        @pl.when(number >= 2)
        def _():
            plan.add_prolonged(cur, prev, get(keep, 0), True)
            wide = number == 2
            sweep(number - 1, jnp.where(wide, 0, 16),
                  jnp.where(wide, plan.rows // BLOCK, (plan.rows - 32) // BLOCK))
            put(keep, 3, plan.restricted(cur, prev, tile_index))

        @pl.when(number == 2)
        def _():
            put(send, 0, get(keep, 3))
            correction = get(keep, 1)
            put(keep, 3, plus(get(keep, 3), correction))
            plan.add_prolonged(cur, prev, correction, False)
            sweep(2, 16, (plan.rows - 32) // BLOCK)
            put(send, 1, plan.restricted(cur, prev, tile_index))

    return body


def second_kernel(plan):
    def body(meta, ax, loads, table, classes, state, keep, got, out, coef, ccoef, cwork, cur, prev, corr):
        number, tile_index = meta[0], meta[1]
        cur[...] = state[0]
        prev[...] = state[1]
        for g in range(2):
            cwork[g] = jnp.zeros((plan.cbuf, LANES), jnp.float32)
        plan.stiffness(classes, table, coef, ccoef)

        @pl.when(number == 2)
        def _():
            gap = minus(get(got, 0), get(keep, 3))
            put(corr, 0, plan.coarse(gap, cwork, ccoef, tile_index))

        @pl.when(number == 3)
        def _():
            second = plus(get(got, 0), get(keep, 1))
            third = plan.coarse(minus(second, get(keep, 0)), cwork, ccoef, tile_index)
            plan.add_prolonged(cur, prev, third, False)
            plan.sweep(cur, prev, coef, ax, loads, 3, 32, (plan.rows - 64) // BLOCK, tile_index)
            early = plan.coarse(minus(get(keep, 2), second), cwork, ccoef, tile_index)
            gap = minus(plus(early, get(got, 1)), plus(get(keep, 3), third))
            put(corr, 0, plan.coarse(gap, cwork, ccoef, tile_index))

        @pl.when(number >= 2)
        def _():
            plan.add_prolonged(cur, prev, get(corr, 0), False)

        def one(j, carry):
            r = pl.multiple_of(j * 16, 16)
            place = pl.multiple_of(MARGIN + REACH + r, 8)
            now = [cur[a, pl.ds(place, 16), :] for a in range(GROUPS)]
            speed = [(now[a] - prev[a, pl.ds(place, 16), :]) * (1.0 / TIME_STEP) for a in range(GROUPS)]
            for f, pieces in enumerate((interleave(now), interleave(speed))):
                for q in range(GROUPS):
                    out[0, f, pl.ds(r, 16), q * LANES : (q + 1) * LANES] = pieces[q]
            return carry

        lax.fori_loop(0, plan.tile // 16, one, 0)

    return body


def paired_plan(mesh):
    slices, tiles = mesh.shape["tm"], mesh.shape["span"]

    def joint(slice_number, tile_index):
        return slice_number * tiles + tile_index

    def exchange(first):
        pairs = []
        for k in range(slices):
            for s in range(tiles):
                partner = s + 1 if (s - first) % 2 == 0 else s - 1
                if 0 <= partner < tiles:
                    pairs.append((joint(k, s), joint(k, partner)))
                else:
                    pairs.append((joint(k, s), joint(k ^ 1, s)))
        return pairs

    swap = [(k, k ^ 1) for k in range(slices)]
    smem = pl.BlockSpec(memory_space=pltpu.SMEM)
    vmem = pl.BlockSpec(memory_space=pltpu.VMEM)
    params = pltpu.CompilerParams(vmem_limit_bytes=40 * 2**20)

    def on_pair(start_state, stiff_class, class_stiffness, axle_rows, axle_cols, axle_class, load_table):
        tile_rows = start_state.shape[1]
        steps, axles = axle_rows.shape
        plan = Plan(tile_rows, tiles, steps, axles)
        number = lax.axis_index("tm")
        tile_index = lax.axis_index("span")
        even = (tile_index & 1) == 0
        low, high = 0, tile_rows - REACH
        to_one = lax.dynamic_slice_in_dim(start_state, jnp.where(even, high, low), REACH, axis=1)
        to_other = lax.dynamic_slice_in_dim(start_state, jnp.where(even, low, high), REACH, axis=1)
        one_side = lax.ppermute(to_one, ("tm", "span"), exchange(0))
        other_side = lax.ppermute(to_other, ("tm", "span"), exchange(1))
        own_axles = jnp.stack([axle_rows, axle_cols, axle_class]).reshape(-1)
        ax = lax.all_gather(own_axles, "tm").reshape(-1)
        meta = jnp.stack([number, tile_index]).astype(jnp.int32)
        classes = stiff_class.reshape(1, -1)
        f32 = jnp.float32
        coarse = (2, 2, plan.crows, LANES)
        common = [
            pltpu.VMEM((3, GROUPS, 8, LANES), f32),
            pltpu.VMEM((2, 8, LANES), f32),
            pltpu.VMEM((2, plan.cbuf, LANES), f32),
        ]
        state, send, keep = pl.pallas_call(
            first_kernel(plan),
            out_shape=(
                jax.ShapeDtypeStruct((2, GROUPS, plan.buf, LANES), f32),
                jax.ShapeDtypeStruct((2,) + coarse, f32),
                jax.ShapeDtypeStruct((4,) + coarse, f32),
            ),
            in_specs=[smem] * 4 + [vmem] * 4,
            out_specs=(vmem, vmem, vmem),
            scratch_shapes=common + [pltpu.VMEM((2, plan.cbuf, LANES), f32)],
            compiler_params=params,
        )(meta, ax, load_table, class_stiffness, classes, start_state, one_side, other_side)
        got = lax.ppermute(send, "tm", swap)
        return pl.pallas_call(
            second_kernel(plan),
            out_shape=jax.ShapeDtypeStruct((1,) + start_state.shape, f32),
            in_specs=[smem] * 4 + [vmem] * 4,
            out_specs=vmem,
            scratch_shapes=common
            + [pltpu.VMEM((GROUPS, plan.buf, LANES), f32)] * 2
            + [pltpu.VMEM((1,) + coarse, f32)],
            compiler_params=params,
        )(meta, ax, load_table, class_stiffness, classes, state, keep, got)

    return on_pair


def solution(mesh):
    in_specs = (
        P(None, ("parts", "span"), None),
        P("parts"),
        P(),
        P(("parts", "tm"), None),
        P(("parts", "tm"), None),
        P(("parts", "tm"), None),
        P(),
    )
    out_specs = P("tm", None, ("parts", "span"), None)
    body = paired_plan(mesh) if mesh.shape["tm"] == SLICES else on_device
    return jax.shard_map(body, mesh=mesh, in_specs=in_specs, out_specs=out_specs, check_vma=False)
```

```python
import jax
import jax.numpy as jnp
from jax import lax
from jax.experimental import pallas as pl
from jax.experimental.pallas import tpu as pltpu
from jax.sharding import PartitionSpec as P

TIME_STEP = 0.2
DAMPING = 0.05
TWIST = 0.5
CROSS_STIFF = 1.0
COARSE_SPACING = 256.0


def extended(cells, sides, width):
    for axis, dim in sides:
        count = lax.axis_size(axis)
        ends = count - 1
        head = lax.slice_in_dim(cells, 0, width, axis=dim)
        tail = lax.slice_in_dim(cells, cells.shape[dim] - width, cells.shape[dim], axis=dim)
        cells = jnp.concatenate(
            [
                lax.ppermute(tail, axis, [(i, (i + 1) % count) for i in range(ends)]),
                cells,
                lax.ppermute(head, axis, [((i + 1) % count, i) for i in range(ends)]),
            ],
            axis=dim,
        )
    return cells


def shifted(value, axis, steps):
    count = lax.axis_size(axis)
    leading, last = (max(0, -steps), min(count, count - steps))
    return lax.ppermute(value, axis, [(source, source + steps) for source in range(leading, last)])


def stiffness_term(padded, column_stiff):
    widened = jnp.pad(padded, ((0, 0), (2, 2)))
    along_rows = widened[2:] - 2.0 * widened[1:-1] + widened[:-2]
    along_four = along_rows[2:] - 2.0 * along_rows[1:-1] + along_rows[:-2]
    across = widened[:, 2:] - 2.0 * widened[:, 1:-1] + widened[:, :-2]
    across_four = across[:, 2:] - 2.0 * across[:, 1:-1] + across[:, :-2]
    mixed_term = across[2:] - 2.0 * across[1:-1] + across[:-2]
    return (
        column_stiff * along_four[:, 2:-2]
        + 2.0 * TWIST * mixed_term[1:-1, 1:-1]
        + CROSS_STIFF * across_four[2:-2]
    )


def advance(padded, deflect, velocity, column_stiff, loading, spacing, time_step):
    velocity = (1.0 - time_step * DAMPING) * velocity + time_step * (
        loading - stiffness_term(padded, column_stiff) / spacing
    )
    return (deflect + time_step * velocity, velocity)


def restrict(fine_field):
    leading = fine_field.shape[:-2]
    row_count = fine_field.shape[-2]
    col_count = fine_field.shape[-1]
    return jnp.mean(
        fine_field.reshape(leading + (row_count // 4, 4, col_count // 4, 4)), axis=(-3, -1)
    )


def prolong(coarse):
    return jnp.repeat(jnp.repeat(coarse, 4, axis=-2), 4, axis=-1)


def table_lookup(indices, table):
    entries = table.shape[0]
    matches = indices[..., None] == lax.iota(jnp.int32, entries)
    return jnp.sum(jnp.where(matches, table, 0.0), axis=-1)


def point_loads(axle_row, axle_col, weights, first_row, row_total, col_total):
    row_hot = jnp.where(
        axle_row[:, None] - first_row == lax.iota(jnp.int32, row_total)[None, :],
        weights[:, None],
        0.0,
    )
    col_hot = jnp.where(axle_col[:, None] == lax.iota(jnp.int32, col_total)[None, :], 1.0, 0.0)
    return jnp.einsum(
        "ar,ac->rc",
        row_hot,
        col_hot,
        precision=lax.Precision.HIGHEST,
        preferred_element_type=jnp.float32,
    )


def coarse_loading(step_rows, step_cols, weights, first_row, coarse_count, coarse_cols):
    step_total = step_rows.shape[0]
    scaled = weights.reshape(-1) / (16.0 * step_total)
    return point_loads(
        step_rows.reshape(-1) // 4,
        step_cols.reshape(-1) // 4,
        scaled,
        first_row,
        coarse_count,
        coarse_cols,
    )


def on_device(
    start_state, stiff_class, class_stiffness, axle_rows, axle_cols, axle_class, load_table
):
    slice_count = lax.axis_size("tm")
    tile_index = lax.axis_index("span")
    slice_index = lax.axis_index("tm")
    tile_rows = start_state.shape[1]
    width = start_state.shape[2]
    coarse_cols = width // 4
    fine_steps = axle_rows.shape[0]
    coarse_first = tile_index * (tile_rows // 4)
    coarse_count = tile_rows // 4
    column_stiff = table_lookup(stiff_class, class_stiffness)
    coarse_stiff = jnp.mean(column_stiff.reshape(coarse_cols, 4), axis=-1)
    weights = table_lookup(axle_class, load_table)
    own_loading = coarse_loading(
        axle_rows, axle_cols, weights, coarse_first, coarse_count, coarse_cols
    )
    coarse_tau = TIME_STEP * fine_steps

    def coarse_step(fields, loading):
        padded = extended(fields[0], (("span", 0),), 2)
        deflect, velocity = advance(
            padded, fields[0], fields[1], coarse_stiff, loading, COARSE_SPACING, coarse_tau
        )
        return jnp.stack([deflect, velocity])

    def relay(anchor, correction):

        def one_round(round_index, current):
            advanced = coarse_step(current, own_loading)
            if correction is not None:
                advanced = advanced + correction
            moved = shifted(advanced, "tm", 1)
            return jnp.where(slice_index == 0, anchor, moved)

        return lax.fori_loop(0, slice_count - 1, one_round, anchor)

    def fine_sweep(fields):
        deflect, velocity = (fields[0], fields[1])
        first_row = tile_index * tile_rows
        for substep in range(fine_steps):
            padded = extended(deflect, (("span", 0),), 2)
            loading = point_loads(
                axle_rows[substep],
                axle_cols[substep],
                weights[substep],
                first_row,
                tile_rows,
                width,
            )
            deflect, velocity = advance(
                padded, deflect, velocity, column_stiff, loading, 1.0, TIME_STEP
            )
        return jnp.stack([deflect, velocity])

    anchor = restrict(start_state)
    first_chain = relay(anchor, None)
    first_old = coarse_step(first_chain, own_loading)
    start_zero = jnp.where(slice_index == 0, start_state, prolong(first_chain))
    sweep_zero = fine_sweep(start_zero)
    second_chain = relay(anchor, restrict(sweep_zero) - first_old)
    second_old = coarse_step(second_chain, own_loading)
    prior = shifted(sweep_zero, "tm", 1)
    start_one = jnp.where(
        slice_index == 0, start_state, prior + prolong(second_chain - restrict(prior))
    )
    sweep_one = fine_sweep(start_one)
    third_correction = restrict(sweep_one) - second_old
    third_chain = relay(anchor, third_correction)
    following = coarse_step(third_chain, own_loading) + third_correction
    end_state = sweep_one + prolong(following - restrict(sweep_one))
    return end_state[None]


SLICES = 4
LANES = 128
GROUPS = 8
MARGIN = 8
REACH = 48
CREACH = REACH // 4
KEPT = 24
RATIO = TIME_STEP * TIME_STEP


def lane_index(rows):
    return lax.broadcasted_iota(jnp.int32, (rows, LANES), 1)


def from_left(x):
    lane = lane_index(x.shape[0])
    source = jnp.where(lane < 8, (lane + 119) % LANES, lane - 8)
    moved = jnp.take_along_axis(x, source, axis=1, mode="promise_in_bounds")
    return jnp.where(lane == 0, 0.0, moved)


def from_right(x):
    lane = lane_index(x.shape[0])
    source = jnp.where(lane >= 120, (lane + 9) % LANES, lane + 8)
    moved = jnp.take_along_axis(x, source, axis=1, mode="promise_in_bounds")
    return jnp.where(lane == LANES - 1, 0.0, moved)


def interleave(pieces):
    pieces = list(pieces)
    lane = lane_index(pieces[0].shape[0])
    for dist in (1, 2, 4):
        keep = (lane & dist) == 0
        for low in range(GROUPS):
            if low & dist:
                continue
            high = low + dist
            first, second = pieces[low], pieces[high]
            pieces[low] = jnp.where(keep, first, pltpu.roll(second, dist, 1))
            pieces[high] = jnp.where(keep, pltpu.roll(first, LANES - dist, 1), second)
    return pieces


def tall(row_vreg, rows):
    return jnp.concatenate([row_vreg] * (rows // 8), axis=0)


class Plan:
    def __init__(self, tile_rows, span, steps, axles):
        self.tile = tile_rows
        self.rows = tile_rows + 2 * REACH
        self.buf = self.rows + 2 * MARGIN
        self.crows = self.rows // 4
        self.cbuf = self.crows + 2 * MARGIN
        self.span = span
        self.steps = steps
        self.axles = axles
        self.coarse_tau = TIME_STEP * steps

    def stiffness(self, classes_ref, table_ref, coef, ccoef):
        entries = table_ref.shape[0]
        pieces = []
        for q in range(GROUPS):
            cls = jnp.broadcast_to(classes_ref[:, q * LANES : (q + 1) * LANES], (8, LANES))
            value = jnp.zeros((8, LANES), jnp.float32)
            for entry in range(entries):
                value = jnp.where(cls == entry, table_ref[entry], value)
            pieces.append(value)
        stiff = interleave(pieces)
        for a in range(GROUPS):
            s = stiff[a]
            coef[0, a] = (2.0 - TIME_STEP * DAMPING) - RATIO * (6.0 * s + 10.0)
            coef[1, a] = RATIO * (4.0 * s + 2.0)
            coef[2, a] = -RATIO * s
        for g in range(2):
            ccoef[g] = 0.25 * (stiff[4 * g] + stiff[4 * g + 1] + stiff[4 * g + 2] + stiff[4 * g + 3])

    def clear_outside(self, ref, tile_index):
        @pl.when(tile_index == 0)
        def _():
            for a in range(GROUPS):
                ref[a, pl.ds(MARGIN + REACH - 8, 8), :] = jnp.zeros((8, LANES), jnp.float32)

        @pl.when(tile_index == self.span - 1)
        def _():
            for a in range(GROUPS):
                ref[a, pl.ds(MARGIN + REACH + self.tile, 8), :] = jnp.zeros((8, LANES), jnp.float32)

    def block(self, src, dst, coef, r0, size):
        def at(a, offset):
            return src[a, pl.ds(r0 + offset, size), :]

        w, s1, t = {}, {}, {}

        def make(a):
            w[a] = at(a, 0)
            s1[a] = at(a, -1) + at(a, 1)
            t[a] = s1[a] - 6.0 * w[a]

        for a in (6, 7, 0, 1):
            make(a)
        w[-2], w[-1], t[-1] = from_left(w[6]), from_left(w[7]), from_left(t[7])
        w[8], w[9], t[8] = from_right(w[0]), from_right(w[1]), from_right(t[0])
        for a in range(GROUPS):
            if a + 2 not in w:
                make(a + 2)
            s2 = at(a, -2) + at(a, 2)
            across = (t[a - 1] + t[a + 1]) + (w[a - 2] + w[a + 2])
            along = tall(coef[2, a], size) * s2 + tall(coef[1, a], size) * s1[a]
            along = along + tall(coef[0, a], size) * w[a]
            old = dst[a, pl.ds(r0, size), :]
            dst[a, pl.ds(r0, size), :] = along - RATIO * across - (1.0 - TIME_STEP * DAMPING) * old

    def axle(self, ax, loads, number, step, i):
        per = self.steps * self.axles
        base = number * (3 * per) + step * self.axles + i
        return ax[base], ax[base + per], loads[ax[base + 2 * per]]

    def sweep(self, cur, prev, coef, ax, loads, number, wanted, tile_index):
        origin = tile_index * self.tile - REACH

        def advance_once(src, dst, step, around):
            half = self.tile // 2 + around
            for first in (MARGIN + REACH - around, MARGIN + REACH - around + half):
                self.block(src, dst, coef, first, half)
            lane = lane_index(1)
            for i in range(self.axles):
                row, col, weight = self.axle(ax, loads, number, step, i)
                local = row - origin
                inside = jnp.logical_and(local >= 0, local < self.rows)
                force = jnp.where(inside, RATIO * weight, 0.0)
                place = jnp.where(inside, local, 0) + MARGIN
                where = ((col >> 3) & 15) * 8 + (col >> 7)
                group = col & 7
                here = dst[group, pl.ds(place, 1), :]
                dst[group, pl.ds(place, 1), :] = here + jnp.where(lane == where, force, 0.0)
            self.clear_outside(dst, tile_index)

        for first in range(0, self.steps, 4):
            around = wanted + 2 * (self.steps - first)

            def two(half, carry):
                advance_once(cur, prev, 2 * half, around)
                advance_once(prev, cur, 2 * half + 1, around)
                return carry

            lax.fori_loop(first // 2, first // 2 + 2, two, 0)

    def move_state(self, state, cur, prev, sems, out):
        place = pl.ds(MARGIN + REACH - KEPT, self.tile + 2 * KEPT)
        copies = []
        for f, ref in enumerate((cur, prev)):
            ends = (ref.at[:, place, :], state.at[f])
            copies.append(pltpu.make_async_copy(*(ends if out else ends[::-1]), sems.at[f]))
        for copy in copies:
            copy.start()
        for copy in copies:
            copy.wait()

    def inside(self, tile_index):
        row = lax.broadcasted_iota(jnp.int32, (self.crows, LANES), 0)
        row = row + (tile_index * (self.tile // 4) - CREACH)
        return jnp.logical_and(row >= 0, row < self.span * (self.tile // 4))

    def restricted(self, cur, prev, tile_index):
        keep = self.inside(tile_index)
        fields = []
        for ref in (cur, prev):
            halves = []
            for g in range(2):
                total = None
                for a in range(4 * g, 4 * g + 4):
                    for j in range(4):
                        piece = ref[a, pl.ds(MARGIN + j, self.crows, stride=4), :]
                        total = piece if total is None else total + piece
                halves.append(jnp.where(keep, total * 0.0625, 0.0))
            fields.append(halves)
        now, before = fields
        return now, [now[g] - before[g] for g in range(2)]

    def add_prolonged(self, cur, prev, field, fresh):
        now, change = field
        for g in range(2):
            before = now[g] - change[g]
            for a in range(4 * g, 4 * g + 4):
                for j in range(4):
                    place = pl.ds(MARGIN + j, self.crows, stride=4)
                    if fresh:
                        cur[a, place, :] = now[g]
                        prev[a, place, :] = before
                    else:
                        cur[a, place, :] = cur[a, place, :] + now[g]
                        prev[a, place, :] = prev[a, place, :] + before

    def coarse_loads(self, cload, ax, loads, number, tile_index):
        origin = tile_index * (self.tile // 4) - CREACH
        for g in range(2):
            cload[g] = jnp.zeros((self.cbuf, LANES), jnp.float32)
        lane = lane_index(1)
        scale = TIME_STEP * self.coarse_tau / (16.0 * self.steps)

        def one_step(step, carry):
            for i in range(self.axles):
                row, col, weight = self.axle(ax, loads, number, step, i)
                local = (row >> 2) - origin
                inside = jnp.logical_and(local >= 0, local < self.crows)
                force = jnp.where(inside, scale * weight, 0.0)
                place = jnp.where(inside, local, 0) + MARGIN
                where = ((col >> 3) & 15) * 8 + (col >> 7)
                group = (col >> 2) & 1
                here = cload[group, pl.ds(place, 1), :]
                cload[group, pl.ds(place, 1), :] = here + jnp.where(lane == where, force, 0.0)
            return carry

        lax.fori_loop(0, self.steps, one_step, 0)

    def coarse(self, field, cwork, ccoef, tile_index, cload=None):
        now, change = field
        rows = self.crows
        for g in range(2):
            cwork[g, pl.ds(MARGIN, rows), :] = now[g]

        def at(g, offset):
            return cwork[g, pl.ds(MARGIN + offset, rows), :]

        keep = self.inside(tile_index)
        w = now
        s1 = [at(g, -1) + at(g, 1) for g in range(2)]
        s2 = [at(g, -2) + at(g, 2) for g in range(2)]
        t = [s1[g] - 6.0 * w[g] for g in range(2)]
        left, right = [from_left(t[1]), t[0]], [t[1], from_right(t[0])]
        kappa = TIME_STEP * self.coarse_tau / COARSE_SPACING
        grown, moved = [], []
        for g in range(2):
            s = tall(ccoef[g], rows)
            across = (left[g] + right[g]) + (from_left(w[g]) + from_right(w[g]))
            stiff = across + s * s2[g] - (4.0 * s + 2.0) * s1[g] + (6.0 * s + 10.0) * w[g]
            value = (1.0 - self.coarse_tau * DAMPING) * change[g] - kappa * stiff
            if cload is not None:
                value = value + cload[g, pl.ds(MARGIN, rows), :]
            value = jnp.where(keep, value, 0.0)
            moved.append(value)
            grown.append(w[g] + (self.coarse_tau / TIME_STEP) * value)
        return grown, moved


def put(ref, slot, field):
    for f in range(2):
        for g in range(2):
            ref[slot, f, g] = field[f][g]


def get(ref, slot):
    return [[ref[slot, f, g] for g in range(2)] for f in range(2)]


def plus(x, y):
    return [[x[f][g] + y[f][g] for g in range(2)] for f in range(2)]


def minus(x, y):
    return [[x[f][g] - y[f][g] for g in range(2)] for f in range(2)]


def first_kernel(plan):
    def body(meta, ax, loads, table, classes, own, mine, other, state, send, keep, coef, ccoef, cwork,
             cur, prev, cload, sems):
        number, tile_index = meta[0], meta[1]
        plan.stiffness(classes, table, coef, ccoef)
        for g in range(2):
            cwork[g] = jnp.zeros((plan.cbuf, LANES), jnp.float32)
        for a in range(GROUPS):
            for ref in (cur, prev):
                ref[a, pl.ds(0, MARGIN), :] = jnp.zeros((MARGIN, LANES), jnp.float32)
                ref[a, pl.ds(MARGIN + plan.rows, MARGIN), :] = jnp.zeros((MARGIN, LANES), jnp.float32)

        def load_rows(ref, offset, count):
            half = count // 2

            def one(j, carry):
                r = pl.multiple_of(j * half, 8)
                fields = []
                for f in range(2):
                    fields.append(interleave(
                        [ref[f, pl.ds(r, half), q * LANES : (q + 1) * LANES] for q in range(GROUPS)]))
                place = pl.multiple_of(MARGIN + offset + r, 8)
                for a in range(GROUPS):
                    cur[a, pl.ds(place, half), :] = fields[0][a]
                    prev[a, pl.ds(place, half), :] = fields[0][a] - TIME_STEP * fields[1][a]
                return carry

            lax.fori_loop(0, 2, one, 0)

        even = ((tile_index + number) & 1) == 0
        load_rows(own, REACH, plan.tile)
        load_rows(mine, jnp.where(even, REACH + plan.tile, 0), REACH)
        load_rows(other, jnp.where(even, 0, REACH + plan.tile), REACH)
        plan.clear_outside(cur, tile_index)
        plan.clear_outside(prev, tile_index)
        send[...] = jnp.zeros(send.shape, jnp.float32)

        def sweep(slice_number, wanted):
            plan.sweep(cur, prev, coef, ax, loads, slice_number, wanted, tile_index)

        @pl.when(number >= 2)
        def _():
            put(keep, 0, plan.restricted(cur, prev, tile_index))

        sweep(0, 32)

        @pl.when(number >= 2)
        def _():
            plan.coarse_loads(cload, ax, loads, 0, tile_index)
            chain = plan.coarse(get(keep, 0), cwork, ccoef, tile_index, cload)
            put(keep, 0, chain)
            gap = minus(plan.restricted(cur, prev, tile_index), chain)
            put(keep, 1, plan.coarse(gap, cwork, ccoef, tile_index))

        @pl.when(number == 3)
        def _():
            plan.coarse_loads(cload, ax, loads, 1, tile_index)
            put(keep, 0, plan.coarse(get(keep, 0), cwork, ccoef, tile_index, cload))

        @pl.when((number & 1) == 1)
        def _():
            sweep(1, 16)

        @pl.when(number == 3)
        def _():
            restricted = plan.restricted(cur, prev, tile_index)
            put(send, 0, restricted)
            put(keep, 2, restricted)

        @pl.when(number == 3)
        def _():
            plan.add_prolonged(cur, prev, get(keep, 0), True)
            sweep(2, 16)
            put(keep, 3, plan.restricted(cur, prev, tile_index))

        @pl.when(number == 2)
        def _():
            plan.add_prolonged(cur, prev, get(keep, 0), True)
            sweep(1, 24)
            restricted = plan.restricted(cur, prev, tile_index)
            put(send, 0, restricted)
            correction = get(keep, 1)
            put(keep, 3, plus(restricted, correction))
            plan.add_prolonged(cur, prev, correction, False)
            sweep(2, 8)
            put(send, 1, plan.restricted(cur, prev, tile_index))

        plan.move_state(state, cur, prev, sems, True)

    return body


def second_kernel(plan):
    def body(meta, ax, loads, table, classes, state, keep, got, out, coef, ccoef, cwork, cur, prev,
             corr, sems):
        number, tile_index = meta[0], meta[1]
        plan.move_state(state, cur, prev, sems, False)
        for g in range(2):
            cwork[g] = jnp.zeros((plan.cbuf, LANES), jnp.float32)
        plan.stiffness(classes, table, coef, ccoef)

        @pl.when(number == 2)
        def _():
            gap = minus(get(got, 0), get(keep, 3))
            put(corr, 0, plan.coarse(gap, cwork, ccoef, tile_index))

        @pl.when(number == 3)
        def _():
            second = plus(get(got, 0), get(keep, 1))
            third = plan.coarse(minus(second, get(keep, 0)), cwork, ccoef, tile_index)
            plan.add_prolonged(cur, prev, third, False)
            plan.sweep(cur, prev, coef, ax, loads, 3, 0, tile_index)
            early = plan.coarse(minus(get(keep, 2), second), cwork, ccoef, tile_index)
            gap = minus(plus(early, get(got, 1)), plus(get(keep, 3), third))
            put(corr, 0, plan.coarse(gap, cwork, ccoef, tile_index))

        @pl.when(number >= 2)
        def _():
            plan.add_prolonged(cur, prev, get(corr, 0), False)

        def one(j, carry):
            r = pl.multiple_of(j * 16, 16)
            place = pl.multiple_of(MARGIN + REACH + r, 8)
            now = [cur[a, pl.ds(place, 16), :] for a in range(GROUPS)]
            speed = [(now[a] - prev[a, pl.ds(place, 16), :]) * (1.0 / TIME_STEP) for a in range(GROUPS)]
            for f, pieces in enumerate((interleave(now), interleave(speed))):
                for q in range(GROUPS):
                    out[0, f, pl.ds(r, 16), q * LANES : (q + 1) * LANES] = pieces[q]
            return carry

        lax.fori_loop(0, plan.tile // 16, one, 0)

    return body


def paired_plan(mesh):
    slices, tiles = mesh.shape["tm"], mesh.shape["span"]

    def joint(slice_number, tile_index):
        return slice_number * tiles + tile_index

    halos = []
    for k in range(slices):
        for s in range(tiles):
            partner = s + 1 if (s + k) % 2 == 0 else s - 1
            target = joint(k, partner) if 0 <= partner < tiles else joint(k ^ 2, s)
            halos.append((joint(k, s), target))
    swap = [(k, k ^ 1) for k in range(slices)]
    smem = pl.BlockSpec(memory_space=pltpu.SMEM)
    vmem = pl.BlockSpec(memory_space=pltpu.VMEM)
    hbm = pl.BlockSpec(memory_space=pl.ANY)
    params = pltpu.CompilerParams(vmem_limit_bytes=40 * 2**20)

    def on_pair(start_state, stiff_class, class_stiffness, axle_rows, axle_cols, axle_class, load_table):
        tile_rows = start_state.shape[1]
        steps, axles = axle_rows.shape
        plan = Plan(tile_rows, tiles, steps, axles)
        number = lax.axis_index("tm")
        tile_index = lax.axis_index("span")
        even = ((tile_index + number) & 1) == 0
        edge = lax.dynamic_slice_in_dim(
            start_state, jnp.where(even, tile_rows - REACH, 0), REACH, axis=1)
        mine = lax.ppermute(edge, ("tm", "span"), halos)
        own_axles = jnp.stack([axle_rows, axle_cols, axle_class]).reshape(-1)
        ax = lax.all_gather(own_axles, "tm").reshape(-1)
        mine, ax = lax.optimization_barrier((mine, ax))
        other = lax.ppermute(mine, "tm", swap)
        meta = jnp.stack([number, tile_index]).astype(jnp.int32)
        classes = stiff_class.reshape(1, -1)
        f32 = jnp.float32
        coarse = (2, 2, plan.crows, LANES)
        common = [
            pltpu.VMEM((3, GROUPS, 8, LANES), f32),
            pltpu.VMEM((2, 8, LANES), f32),
            pltpu.VMEM((2, plan.cbuf, LANES), f32),
            pltpu.VMEM((GROUPS, plan.buf, LANES), f32),
            pltpu.VMEM((GROUPS, plan.buf, LANES), f32),
        ]
        state, send, keep = pl.pallas_call(
            first_kernel(plan),
            out_shape=(
                jax.ShapeDtypeStruct((2, GROUPS, tile_rows + 2 * KEPT, LANES), f32),
                jax.ShapeDtypeStruct((2,) + coarse, f32),
                jax.ShapeDtypeStruct((4,) + coarse, f32),
            ),
            in_specs=[smem] * 4 + [vmem] * 4,
            out_specs=(hbm, vmem, vmem),
            scratch_shapes=common + [pltpu.VMEM((2, plan.cbuf, LANES), f32), pltpu.SemaphoreType.DMA((2,))],
            compiler_params=params,
        )(meta, ax, load_table, class_stiffness, classes, start_state, mine, other)
        got = lax.ppermute(send, "tm", swap)
        return pl.pallas_call(
            second_kernel(plan),
            out_shape=jax.ShapeDtypeStruct((1,) + start_state.shape, f32),
            in_specs=[smem] * 4 + [vmem, hbm, vmem, vmem],
            out_specs=vmem,
            scratch_shapes=common + [pltpu.VMEM((1,) + coarse, f32), pltpu.SemaphoreType.DMA((2,))],
            compiler_params=params,
        )(meta, ax, load_table, class_stiffness, classes, state, keep, got)

    return on_pair


def solution(mesh):
    in_specs = (
        P(None, ("parts", "span"), None),
        P("parts"),
        P(),
        P(("parts", "tm"), None),
        P(("parts", "tm"), None),
        P(("parts", "tm"), None),
        P(),
    )
    out_specs = P("tm", None, ("parts", "span"), None)
    body = paired_plan(mesh) if mesh.shape["tm"] == SLICES else on_device
    return jax.shard_map(body, mesh=mesh, in_specs=in_specs, out_specs=out_specs, check_vma=False)
```

```python
import jax
import jax.numpy as jnp
from jax import lax
from jax.experimental import pallas as pl
from jax.experimental.pallas import tpu as pltpu
from jax.sharding import PartitionSpec as P

TIME_STEP = 0.2
DAMPING = 0.05
TWIST = 0.5
CROSS_STIFF = 1.0
COARSE_SPACING = 256.0


def extended(cells, sides, width):
    for axis, dim in sides:
        count = lax.axis_size(axis)
        ends = count - 1
        head = lax.slice_in_dim(cells, 0, width, axis=dim)
        tail = lax.slice_in_dim(cells, cells.shape[dim] - width, cells.shape[dim], axis=dim)
        cells = jnp.concatenate(
            [
                lax.ppermute(tail, axis, [(i, (i + 1) % count) for i in range(ends)]),
                cells,
                lax.ppermute(head, axis, [((i + 1) % count, i) for i in range(ends)]),
            ],
            axis=dim,
        )
    return cells


def shifted(value, axis, steps):
    count = lax.axis_size(axis)
    leading, last = (max(0, -steps), min(count, count - steps))
    return lax.ppermute(value, axis, [(source, source + steps) for source in range(leading, last)])


def stiffness_term(padded, column_stiff):
    widened = jnp.pad(padded, ((0, 0), (2, 2)))
    along_rows = widened[2:] - 2.0 * widened[1:-1] + widened[:-2]
    along_four = along_rows[2:] - 2.0 * along_rows[1:-1] + along_rows[:-2]
    across = widened[:, 2:] - 2.0 * widened[:, 1:-1] + widened[:, :-2]
    across_four = across[:, 2:] - 2.0 * across[:, 1:-1] + across[:, :-2]
    mixed_term = across[2:] - 2.0 * across[1:-1] + across[:-2]
    return (
        column_stiff * along_four[:, 2:-2]
        + 2.0 * TWIST * mixed_term[1:-1, 1:-1]
        + CROSS_STIFF * across_four[2:-2]
    )


def advance(padded, deflect, velocity, column_stiff, loading, spacing, time_step):
    velocity = (1.0 - time_step * DAMPING) * velocity + time_step * (
        loading - stiffness_term(padded, column_stiff) / spacing
    )
    return (deflect + time_step * velocity, velocity)


def restrict(fine_field):
    leading = fine_field.shape[:-2]
    row_count = fine_field.shape[-2]
    col_count = fine_field.shape[-1]
    return jnp.mean(
        fine_field.reshape(leading + (row_count // 4, 4, col_count // 4, 4)), axis=(-3, -1)
    )


def prolong(coarse):
    return jnp.repeat(jnp.repeat(coarse, 4, axis=-2), 4, axis=-1)


def table_lookup(indices, table):
    entries = table.shape[0]
    matches = indices[..., None] == lax.iota(jnp.int32, entries)
    return jnp.sum(jnp.where(matches, table, 0.0), axis=-1)


def point_loads(axle_row, axle_col, weights, first_row, row_total, col_total):
    row_hot = jnp.where(
        axle_row[:, None] - first_row == lax.iota(jnp.int32, row_total)[None, :],
        weights[:, None],
        0.0,
    )
    col_hot = jnp.where(axle_col[:, None] == lax.iota(jnp.int32, col_total)[None, :], 1.0, 0.0)
    return jnp.einsum(
        "ar,ac->rc",
        row_hot,
        col_hot,
        precision=lax.Precision.HIGHEST,
        preferred_element_type=jnp.float32,
    )


def coarse_loading(step_rows, step_cols, weights, first_row, coarse_count, coarse_cols):
    step_total = step_rows.shape[0]
    scaled = weights.reshape(-1) / (16.0 * step_total)
    return point_loads(
        step_rows.reshape(-1) // 4,
        step_cols.reshape(-1) // 4,
        scaled,
        first_row,
        coarse_count,
        coarse_cols,
    )


def on_device(
    start_state, stiff_class, class_stiffness, axle_rows, axle_cols, axle_class, load_table
):
    slice_count = lax.axis_size("tm")
    tile_index = lax.axis_index("span")
    slice_index = lax.axis_index("tm")
    tile_rows = start_state.shape[1]
    width = start_state.shape[2]
    coarse_cols = width // 4
    fine_steps = axle_rows.shape[0]
    coarse_first = tile_index * (tile_rows // 4)
    coarse_count = tile_rows // 4
    column_stiff = table_lookup(stiff_class, class_stiffness)
    coarse_stiff = jnp.mean(column_stiff.reshape(coarse_cols, 4), axis=-1)
    weights = table_lookup(axle_class, load_table)
    own_loading = coarse_loading(
        axle_rows, axle_cols, weights, coarse_first, coarse_count, coarse_cols
    )
    coarse_tau = TIME_STEP * fine_steps

    def coarse_step(fields, loading):
        padded = extended(fields[0], (("span", 0),), 2)
        deflect, velocity = advance(
            padded, fields[0], fields[1], coarse_stiff, loading, COARSE_SPACING, coarse_tau
        )
        return jnp.stack([deflect, velocity])

    def relay(anchor, correction):

        def one_round(round_index, current):
            advanced = coarse_step(current, own_loading)
            if correction is not None:
                advanced = advanced + correction
            moved = shifted(advanced, "tm", 1)
            return jnp.where(slice_index == 0, anchor, moved)

        return lax.fori_loop(0, slice_count - 1, one_round, anchor)

    def fine_sweep(fields):
        deflect, velocity = (fields[0], fields[1])
        first_row = tile_index * tile_rows
        for substep in range(fine_steps):
            padded = extended(deflect, (("span", 0),), 2)
            loading = point_loads(
                axle_rows[substep],
                axle_cols[substep],
                weights[substep],
                first_row,
                tile_rows,
                width,
            )
            deflect, velocity = advance(
                padded, deflect, velocity, column_stiff, loading, 1.0, TIME_STEP
            )
        return jnp.stack([deflect, velocity])

    anchor = restrict(start_state)
    first_chain = relay(anchor, None)
    first_old = coarse_step(first_chain, own_loading)
    start_zero = jnp.where(slice_index == 0, start_state, prolong(first_chain))
    sweep_zero = fine_sweep(start_zero)
    second_chain = relay(anchor, restrict(sweep_zero) - first_old)
    second_old = coarse_step(second_chain, own_loading)
    prior = shifted(sweep_zero, "tm", 1)
    start_one = jnp.where(
        slice_index == 0, start_state, prior + prolong(second_chain - restrict(prior))
    )
    sweep_one = fine_sweep(start_one)
    third_correction = restrict(sweep_one) - second_old
    third_chain = relay(anchor, third_correction)
    following = coarse_step(third_chain, own_loading) + third_correction
    end_state = sweep_one + prolong(following - restrict(sweep_one))
    return end_state[None]


SLICES = 4
LANES = 128
GROUPS = 8
MARGIN = 8
REACH = 48
CREACH = REACH // 4
KEPT = 24
RATIO = TIME_STEP * TIME_STEP


def lane_index(rows):
    return lax.broadcasted_iota(jnp.int32, (rows, LANES), 1)


def from_left(x):
    lane = lane_index(x.shape[0])
    source = jnp.where(lane < 8, (lane + 119) % LANES, lane - 8)
    moved = jnp.take_along_axis(x, source, axis=1, mode="promise_in_bounds")
    return jnp.where(lane == 0, 0.0, moved)


def from_right(x):
    lane = lane_index(x.shape[0])
    source = jnp.where(lane >= 120, (lane + 9) % LANES, lane + 8)
    moved = jnp.take_along_axis(x, source, axis=1, mode="promise_in_bounds")
    return jnp.where(lane == LANES - 1, 0.0, moved)


def interleave(pieces):
    pieces = list(pieces)
    lane = lane_index(pieces[0].shape[0])
    for dist in (1, 2, 4):
        keep = (lane & dist) == 0
        for low in range(GROUPS):
            if low & dist:
                continue
            high = low + dist
            first, second = pieces[low], pieces[high]
            pieces[low] = jnp.where(keep, first, pltpu.roll(second, dist, 1))
            pieces[high] = jnp.where(keep, pltpu.roll(first, LANES - dist, 1), second)
    return pieces


def tall(row_vreg, rows):
    return jnp.concatenate([row_vreg] * (rows // 8), axis=0)


class Plan:
    def __init__(self, tile_rows, span, steps, axles):
        self.tile = tile_rows
        self.rows = tile_rows + 2 * REACH
        self.buf = self.rows + 2 * MARGIN
        self.crows = self.rows // 4
        self.cbuf = self.crows + 2 * MARGIN
        self.span = span
        self.steps = steps
        self.axles = axles
        self.coarse_tau = TIME_STEP * steps

    def stiffness(self, classes_ref, table_ref, coef, ccoef):
        entries = table_ref.shape[0]
        pieces = []
        for q in range(GROUPS):
            cls = jnp.broadcast_to(classes_ref[:, q * LANES : (q + 1) * LANES], (8, LANES))
            value = jnp.zeros((8, LANES), jnp.float32)
            for entry in range(entries):
                value = jnp.where(cls == entry, table_ref[entry], value)
            pieces.append(value)
        stiff = interleave(pieces)
        for a in range(GROUPS):
            s = stiff[a]
            coef[0, a] = (2.0 - TIME_STEP * DAMPING) - RATIO * (6.0 * s + 10.0)
            coef[1, a] = RATIO * (4.0 * s + 2.0)
            coef[2, a] = -RATIO * s
        for g in range(2):
            ccoef[g] = 0.25 * (stiff[4 * g] + stiff[4 * g + 1] + stiff[4 * g + 2] + stiff[4 * g + 3])

    def clear_outside(self, ref, tile_index):
        @pl.when(tile_index == 0)
        def _():
            for a in range(GROUPS):
                ref[a, pl.ds(MARGIN + REACH - 8, 8), :] = jnp.zeros((8, LANES), jnp.float32)

        @pl.when(tile_index == self.span - 1)
        def _():
            for a in range(GROUPS):
                ref[a, pl.ds(MARGIN + REACH + self.tile, 8), :] = jnp.zeros((8, LANES), jnp.float32)

    def block(self, src, dst, coef, r0, size):
        def at(a, offset):
            return src[a, pl.ds(r0 + offset, size), :]

        w, s1, t = {}, {}, {}

        def make(a):
            w[a] = at(a, 0)
            s1[a] = at(a, -1) + at(a, 1)
            t[a] = s1[a] - 6.0 * w[a]

        for a in (6, 7, 0, 1):
            make(a)
        w[-2], w[-1], t[-1] = from_left(w[6]), from_left(w[7]), from_left(t[7])
        w[8], w[9], t[8] = from_right(w[0]), from_right(w[1]), from_right(t[0])
        for a in range(GROUPS):
            if a + 2 not in w:
                make(a + 2)
            s2 = at(a, -2) + at(a, 2)
            across = (t[a - 1] + t[a + 1]) + (w[a - 2] + w[a + 2])
            along = tall(coef[2, a], size) * s2 + tall(coef[1, a], size) * s1[a]
            along = along + tall(coef[0, a], size) * w[a]
            old = dst[a, pl.ds(r0, size), :]
            dst[a, pl.ds(r0, size), :] = along - RATIO * across - (1.0 - TIME_STEP * DAMPING) * old

    def add_points(self, ref, ax, force, number, step, origin, limit, coarse):
        base = (number * self.steps + step) * LANES
        clash = ax[base + 4 * self.axles + (1 if coarse else 0)]
        lane = lane_index(1)
        spots = []
        for i in range(self.axles):
            row, group, spot = (ax[base + field * self.axles + i] for field in range(3))
            amount = force[(number * self.steps + step) * self.axles + i]
            if coarse:
                row, group = row >> 2, group >> 2
                amount = amount * (self.coarse_tau / (16.0 * self.steps * TIME_STEP))
            place = jnp.minimum(jnp.maximum(row - origin, -MARGIN), limit + MARGIN - 1) + MARGIN
            spots.append((group, place, jnp.where(lane == spot, amount, 0.0)))

        @pl.when(clash == 0)
        def _():
            before = [ref[group, pl.ds(place, 1), :] for group, place, _ in spots]
            for (group, place, amount), value in zip(spots, before):
                ref[group, pl.ds(place, 1), :] = value + amount

        @pl.when(clash != 0)
        def _():
            for group, place, amount in spots:
                ref[group, pl.ds(place, 1), :] = ref[group, pl.ds(place, 1), :] + amount

    def sweep(self, cur, prev, coef, ax, force, number, wanted, tile_index):
        origin = tile_index * self.tile - REACH

        def advance_once(src, dst, step, around):
            half = self.tile // 2 + around
            for first in (MARGIN + REACH - around, MARGIN + REACH - around + half):
                self.block(src, dst, coef, first, half)
            self.add_points(dst, ax, force, number, step, origin, self.rows, False)
            self.clear_outside(dst, tile_index)

        for first in range(0, self.steps, 4):
            around = wanted + 2 * (self.steps - first)

            def two(half, carry):
                advance_once(cur, prev, 2 * half, around)
                advance_once(prev, cur, 2 * half + 1, around)
                return carry

            lax.fori_loop(first // 2, first // 2 + 2, two, 0)

    def move_state(self, state, cur, prev, sems, out):
        place = pl.ds(MARGIN + REACH - KEPT, self.tile + 2 * KEPT)
        copies = []
        for f, ref in enumerate((cur, prev)):
            ends = (ref.at[:, place, :], state.at[f])
            copies.append(pltpu.make_async_copy(*(ends if out else ends[::-1]), sems.at[f]))
        for copy in copies:
            copy.start()
        for copy in copies:
            copy.wait()

    def inside(self, tile_index):
        row = lax.broadcasted_iota(jnp.int32, (self.crows, LANES), 0)
        row = row + (tile_index * (self.tile // 4) - CREACH)
        return jnp.logical_and(row >= 0, row < self.span * (self.tile // 4))

    def restricted(self, cur, prev, tile_index):
        keep = self.inside(tile_index)
        fields = []
        for ref in (cur, prev):
            halves = []
            for g in range(2):
                total = None
                for a in range(4 * g, 4 * g + 4):
                    for j in range(4):
                        piece = ref[a, pl.ds(MARGIN + j, self.crows, stride=4), :]
                        total = piece if total is None else total + piece
                halves.append(jnp.where(keep, total * 0.0625, 0.0))
            fields.append(halves)
        now, before = fields
        return now, [now[g] - before[g] for g in range(2)]

    def add_prolonged(self, cur, prev, field, fresh):
        now, change = field
        for g in range(2):
            before = now[g] - change[g]
            for a in range(4 * g, 4 * g + 4):
                for j in range(4):
                    place = pl.ds(MARGIN + j, self.crows, stride=4)
                    if fresh:
                        cur[a, place, :] = now[g]
                        prev[a, place, :] = before
                    else:
                        cur[a, place, :] = cur[a, place, :] + now[g]
                        prev[a, place, :] = prev[a, place, :] + before

    def coarse_loads(self, cload, ax, force, number, tile_index):
        origin = tile_index * (self.tile // 4) - CREACH
        for g in range(2):
            cload[g] = jnp.zeros((self.cbuf, LANES), jnp.float32)

        def one_step(step, carry):
            self.add_points(cload, ax, force, number, step, origin, self.crows, True)
            return carry

        lax.fori_loop(0, self.steps, one_step, 0)

    def coarse(self, field, cwork, ccoef, tile_index, cload=None):
        now, change = field
        rows = self.crows
        for g in range(2):
            cwork[g, pl.ds(MARGIN, rows), :] = now[g]

        def at(g, offset):
            return cwork[g, pl.ds(MARGIN + offset, rows), :]

        keep = self.inside(tile_index)
        w = now
        s1 = [at(g, -1) + at(g, 1) for g in range(2)]
        s2 = [at(g, -2) + at(g, 2) for g in range(2)]
        t = [s1[g] - 6.0 * w[g] for g in range(2)]
        left, right = [from_left(t[1]), t[0]], [t[1], from_right(t[0])]
        kappa = TIME_STEP * self.coarse_tau / COARSE_SPACING
        grown, moved = [], []
        for g in range(2):
            s = tall(ccoef[g], rows)
            across = (left[g] + right[g]) + (from_left(w[g]) + from_right(w[g]))
            stiff = across + s * s2[g] - (4.0 * s + 2.0) * s1[g] + (6.0 * s + 10.0) * w[g]
            value = (1.0 - self.coarse_tau * DAMPING) * change[g] - kappa * stiff
            if cload is not None:
                value = value + cload[g, pl.ds(MARGIN, rows), :]
            value = jnp.where(keep, value, 0.0)
            moved.append(value)
            grown.append(w[g] + (self.coarse_tau / TIME_STEP) * value)
        return grown, moved


def put(ref, slot, field):
    for f in range(2):
        for g in range(2):
            ref[slot, f, g] = field[f][g]


def get(ref, slot):
    return [[ref[slot, f, g] for g in range(2)] for f in range(2)]


def plus(x, y):
    return [[x[f][g] + y[f][g] for g in range(2)] for f in range(2)]


def minus(x, y):
    return [[x[f][g] - y[f][g] for g in range(2)] for f in range(2)]


def first_kernel(plan):
    def body(meta, ax, force, table, classes, own, mine, other, state, send, keep, coef, ccoef, cwork,
             cur, prev, cload, sems):
        number, tile_index = meta[0], meta[1]
        plan.stiffness(classes, table, coef, ccoef)
        for g in range(2):
            cwork[g] = jnp.zeros((plan.cbuf, LANES), jnp.float32)
        for a in range(GROUPS):
            for ref in (cur, prev):
                ref[a, pl.ds(0, MARGIN), :] = jnp.zeros((MARGIN, LANES), jnp.float32)
                ref[a, pl.ds(MARGIN + plan.rows, MARGIN), :] = jnp.zeros((MARGIN, LANES), jnp.float32)

        def load_rows(ref, offset, count):
            half = count // 2

            def one(j, carry):
                r = pl.multiple_of(j * half, 8)
                fields = []
                for f in range(2):
                    fields.append(interleave(
                        [ref[f, pl.ds(r, half), q * LANES : (q + 1) * LANES] for q in range(GROUPS)]))
                place = pl.multiple_of(MARGIN + offset + r, 8)
                for a in range(GROUPS):
                    cur[a, pl.ds(place, half), :] = fields[0][a]
                    prev[a, pl.ds(place, half), :] = fields[0][a] - TIME_STEP * fields[1][a]
                return carry

            lax.fori_loop(0, 2, one, 0)

        even = ((tile_index + number) & 1) == 0
        load_rows(own, REACH, plan.tile)
        load_rows(mine, jnp.where(even, REACH + plan.tile, 0), REACH)
        load_rows(other, jnp.where(even, 0, REACH + plan.tile), REACH)
        plan.clear_outside(cur, tile_index)
        plan.clear_outside(prev, tile_index)
        send[...] = jnp.zeros(send.shape, jnp.float32)

        def sweep(slice_number, wanted):
            plan.sweep(cur, prev, coef, ax, force, slice_number, wanted, tile_index)

        @pl.when(number >= 2)
        def _():
            put(keep, 0, plan.restricted(cur, prev, tile_index))

        sweep(0, 32)

        @pl.when(number >= 2)
        def _():
            plan.coarse_loads(cload, ax, force, 0, tile_index)
            chain = plan.coarse(get(keep, 0), cwork, ccoef, tile_index, cload)
            put(keep, 0, chain)
            gap = minus(plan.restricted(cur, prev, tile_index), chain)
            put(keep, 1, plan.coarse(gap, cwork, ccoef, tile_index))

        @pl.when(number == 3)
        def _():
            plan.coarse_loads(cload, ax, force, 1, tile_index)
            put(keep, 0, plan.coarse(get(keep, 0), cwork, ccoef, tile_index, cload))

        @pl.when((number & 1) == 1)
        def _():
            sweep(1, 16)

        @pl.when(number == 3)
        def _():
            restricted = plan.restricted(cur, prev, tile_index)
            put(send, 0, restricted)
            put(keep, 2, restricted)

        @pl.when(number == 3)
        def _():
            plan.add_prolonged(cur, prev, get(keep, 0), True)
            sweep(2, 16)
            put(keep, 3, plan.restricted(cur, prev, tile_index))

        @pl.when(number == 2)
        def _():
            plan.add_prolonged(cur, prev, get(keep, 0), True)
            sweep(1, 24)
            restricted = plan.restricted(cur, prev, tile_index)
            put(send, 0, restricted)
            correction = get(keep, 1)
            put(keep, 3, plus(restricted, correction))
            plan.add_prolonged(cur, prev, correction, False)
            sweep(2, 8)
            put(send, 1, plan.restricted(cur, prev, tile_index))

        plan.move_state(state, cur, prev, sems, True)

    return body


def second_kernel(plan):
    def body(meta, ax, force, table, classes, state, keep, got, out, coef, ccoef, cwork, cur, prev,
             corr, sems):
        number, tile_index = meta[0], meta[1]
        plan.move_state(state, cur, prev, sems, False)
        for g in range(2):
            cwork[g] = jnp.zeros((plan.cbuf, LANES), jnp.float32)
        plan.stiffness(classes, table, coef, ccoef)

        @pl.when(number == 2)
        def _():
            gap = minus(get(got, 0), get(keep, 3))
            put(corr, 0, plan.coarse(gap, cwork, ccoef, tile_index))

        @pl.when(number == 3)
        def _():
            second = plus(get(got, 0), get(keep, 1))
            third = plan.coarse(minus(second, get(keep, 0)), cwork, ccoef, tile_index)
            plan.add_prolonged(cur, prev, third, False)
            plan.sweep(cur, prev, coef, ax, force, 3, 0, tile_index)
            early = plan.coarse(minus(get(keep, 2), second), cwork, ccoef, tile_index)
            gap = minus(plus(early, get(got, 1)), plus(get(keep, 3), third))
            put(corr, 0, plan.coarse(gap, cwork, ccoef, tile_index))

        @pl.when(number >= 2)
        def _():
            plan.add_prolonged(cur, prev, get(corr, 0), False)

        def one(j, carry):
            r = pl.multiple_of(j * 16, 16)
            place = pl.multiple_of(MARGIN + REACH + r, 8)
            now = [cur[a, pl.ds(place, 16), :] for a in range(GROUPS)]
            speed = [(now[a] - prev[a, pl.ds(place, 16), :]) * (1.0 / TIME_STEP) for a in range(GROUPS)]
            for f, pieces in enumerate((interleave(now), interleave(speed))):
                for q in range(GROUPS):
                    out[0, f, pl.ds(r, 16), q * LANES : (q + 1) * LANES] = pieces[q]
            return carry

        lax.fori_loop(0, plan.tile // 16, one, 0)

    return body


def shared_spot(spots):
    count = spots.shape[1]
    same = spots[:, :, None] == spots[:, None, :]
    later = lax.iota(jnp.int32, count)[:, None] < lax.iota(jnp.int32, count)[None, :]
    return jnp.max((same & later).astype(jnp.int32), axis=(1, 2))[:, None]


def paired_plan(mesh):
    slices, tiles = mesh.shape["tm"], mesh.shape["span"]

    def joint(slice_number, tile_index):
        return slice_number * tiles + tile_index

    halos = []
    for k in range(slices):
        for s in range(tiles):
            partner = s + 1 if (s + k) % 2 == 0 else s - 1
            target = joint(k, partner) if 0 <= partner < tiles else joint(k ^ 2, s)
            halos.append((joint(k, s), target))
    swap = [(k, k ^ 1) for k in range(slices)]
    smem = pl.BlockSpec(memory_space=pltpu.SMEM)
    vmem = pl.BlockSpec(memory_space=pltpu.VMEM)
    hbm = pl.BlockSpec(memory_space=pl.ANY)
    params = pltpu.CompilerParams(vmem_limit_bytes=40 * 2**20)

    def on_pair(start_state, stiff_class, class_stiffness, axle_rows, axle_cols, axle_class, load_table):
        tile_rows = start_state.shape[1]
        steps, axles = axle_rows.shape
        plan = Plan(tile_rows, tiles, steps, axles)
        number = lax.axis_index("tm")
        tile_index = lax.axis_index("span")
        even = ((tile_index + number) & 1) == 0
        edge = lax.dynamic_slice_in_dim(
            start_state, jnp.where(even, tile_rows - REACH, 0), REACH, axis=1)
        mine = lax.ppermute(edge, ("tm", "span"), halos)
        group, lane = axle_cols & 7, ((axle_cols >> 3) & 15) * 8 + (axle_cols >> 7)
        own_axles = jnp.concatenate(
            [axle_rows, group, lane, axle_class]
            + [shared_spot(axle_rows * 8 + group), shared_spot((axle_rows >> 2) * 2 + (group >> 2))]
            + [jnp.zeros((steps, LANES - 4 * axles - 2), jnp.int32)],
            axis=1)
        gathered = lax.all_gather(own_axles, "tm")
        mine, gathered = lax.optimization_barrier((mine, gathered))
        ax = gathered.reshape(-1)
        force = RATIO * table_lookup(gathered[:, :, 3 * axles : 4 * axles].reshape(-1), load_table)
        other = lax.ppermute(mine, "tm", swap)
        meta = jnp.stack([number, tile_index]).astype(jnp.int32)
        classes = stiff_class.reshape(1, -1)
        f32 = jnp.float32
        coarse = (2, 2, plan.crows, LANES)
        common = [
            pltpu.VMEM((3, GROUPS, 8, LANES), f32),
            pltpu.VMEM((2, 8, LANES), f32),
            pltpu.VMEM((2, plan.cbuf, LANES), f32),
            pltpu.VMEM((GROUPS, plan.buf, LANES), f32),
            pltpu.VMEM((GROUPS, plan.buf, LANES), f32),
        ]
        state, send, keep = pl.pallas_call(
            first_kernel(plan),
            out_shape=(
                jax.ShapeDtypeStruct((2, GROUPS, tile_rows + 2 * KEPT, LANES), f32),
                jax.ShapeDtypeStruct((2,) + coarse, f32),
                jax.ShapeDtypeStruct((4,) + coarse, f32),
            ),
            in_specs=[smem] * 4 + [vmem] * 4,
            out_specs=(hbm, vmem, vmem),
            scratch_shapes=common + [pltpu.VMEM((2, plan.cbuf, LANES), f32), pltpu.SemaphoreType.DMA((2,))],
            compiler_params=params,
        )(meta, ax, force, class_stiffness, classes, start_state, mine, other)
        got = lax.ppermute(send, "tm", swap)
        return pl.pallas_call(
            second_kernel(plan),
            out_shape=jax.ShapeDtypeStruct((1,) + start_state.shape, f32),
            in_specs=[smem] * 4 + [vmem, hbm, vmem, vmem],
            out_specs=vmem,
            scratch_shapes=common + [pltpu.VMEM((1,) + coarse, f32), pltpu.SemaphoreType.DMA((2,))],
            compiler_params=params,
        )(meta, ax, force, class_stiffness, classes, state, keep, got)

    return on_pair


def solution(mesh):
    in_specs = (
        P(None, ("parts", "span"), None),
        P("parts"),
        P(),
        P(("parts", "tm"), None),
        P(("parts", "tm"), None),
        P(("parts", "tm"), None),
        P(),
    )
    out_specs = P("tm", None, ("parts", "span"), None)
    body = paired_plan(mesh) if mesh.shape["tm"] == SLICES else on_device
    return jax.shard_map(body, mesh=mesh, in_specs=in_specs, out_specs=out_specs, check_vma=False)
```

```python
import jax
import jax.numpy as jnp
from jax import lax
from jax.experimental import pallas as pl
from jax.experimental.pallas import tpu as pltpu
from jax.sharding import PartitionSpec as P

TIME_STEP = 0.2
DAMPING = 0.05
TWIST = 0.5
CROSS_STIFF = 1.0
COARSE_SPACING = 256.0


def extended(cells, sides, width):
    for axis, dim in sides:
        count = lax.axis_size(axis)
        ends = count - 1
        head = lax.slice_in_dim(cells, 0, width, axis=dim)
        tail = lax.slice_in_dim(cells, cells.shape[dim] - width, cells.shape[dim], axis=dim)
        cells = jnp.concatenate(
            [
                lax.ppermute(tail, axis, [(i, (i + 1) % count) for i in range(ends)]),
                cells,
                lax.ppermute(head, axis, [((i + 1) % count, i) for i in range(ends)]),
            ],
            axis=dim,
        )
    return cells


def shifted(value, axis, steps):
    count = lax.axis_size(axis)
    leading, last = (max(0, -steps), min(count, count - steps))
    return lax.ppermute(value, axis, [(source, source + steps) for source in range(leading, last)])


def stiffness_term(padded, column_stiff):
    widened = jnp.pad(padded, ((0, 0), (2, 2)))
    along_rows = widened[2:] - 2.0 * widened[1:-1] + widened[:-2]
    along_four = along_rows[2:] - 2.0 * along_rows[1:-1] + along_rows[:-2]
    across = widened[:, 2:] - 2.0 * widened[:, 1:-1] + widened[:, :-2]
    across_four = across[:, 2:] - 2.0 * across[:, 1:-1] + across[:, :-2]
    mixed_term = across[2:] - 2.0 * across[1:-1] + across[:-2]
    return (
        column_stiff * along_four[:, 2:-2]
        + 2.0 * TWIST * mixed_term[1:-1, 1:-1]
        + CROSS_STIFF * across_four[2:-2]
    )


def advance(padded, deflect, velocity, column_stiff, loading, spacing, time_step):
    velocity = (1.0 - time_step * DAMPING) * velocity + time_step * (
        loading - stiffness_term(padded, column_stiff) / spacing
    )
    return (deflect + time_step * velocity, velocity)


def restrict(fine_field):
    leading = fine_field.shape[:-2]
    row_count = fine_field.shape[-2]
    col_count = fine_field.shape[-1]
    return jnp.mean(
        fine_field.reshape(leading + (row_count // 4, 4, col_count // 4, 4)), axis=(-3, -1)
    )


def prolong(coarse):
    return jnp.repeat(jnp.repeat(coarse, 4, axis=-2), 4, axis=-1)


def table_lookup(indices, table):
    entries = table.shape[0]
    matches = indices[..., None] == lax.iota(jnp.int32, entries)
    return jnp.sum(jnp.where(matches, table, 0.0), axis=-1)


def point_loads(axle_row, axle_col, weights, first_row, row_total, col_total):
    row_hot = jnp.where(
        axle_row[:, None] - first_row == lax.iota(jnp.int32, row_total)[None, :],
        weights[:, None],
        0.0,
    )
    col_hot = jnp.where(axle_col[:, None] == lax.iota(jnp.int32, col_total)[None, :], 1.0, 0.0)
    return jnp.einsum(
        "ar,ac->rc",
        row_hot,
        col_hot,
        precision=lax.Precision.HIGHEST,
        preferred_element_type=jnp.float32,
    )


def coarse_loading(step_rows, step_cols, weights, first_row, coarse_count, coarse_cols):
    step_total = step_rows.shape[0]
    scaled = weights.reshape(-1) / (16.0 * step_total)
    return point_loads(
        step_rows.reshape(-1) // 4,
        step_cols.reshape(-1) // 4,
        scaled,
        first_row,
        coarse_count,
        coarse_cols,
    )


def on_device(
    start_state, stiff_class, class_stiffness, axle_rows, axle_cols, axle_class, load_table
):
    slice_count = lax.axis_size("tm")
    tile_index = lax.axis_index("span")
    slice_index = lax.axis_index("tm")
    tile_rows = start_state.shape[1]
    width = start_state.shape[2]
    coarse_cols = width // 4
    fine_steps = axle_rows.shape[0]
    coarse_first = tile_index * (tile_rows // 4)
    coarse_count = tile_rows // 4
    column_stiff = table_lookup(stiff_class, class_stiffness)
    coarse_stiff = jnp.mean(column_stiff.reshape(coarse_cols, 4), axis=-1)
    weights = table_lookup(axle_class, load_table)
    own_loading = coarse_loading(
        axle_rows, axle_cols, weights, coarse_first, coarse_count, coarse_cols
    )
    coarse_tau = TIME_STEP * fine_steps

    def coarse_step(fields, loading):
        padded = extended(fields[0], (("span", 0),), 2)
        deflect, velocity = advance(
            padded, fields[0], fields[1], coarse_stiff, loading, COARSE_SPACING, coarse_tau
        )
        return jnp.stack([deflect, velocity])

    def relay(anchor, correction):

        def one_round(round_index, current):
            advanced = coarse_step(current, own_loading)
            if correction is not None:
                advanced = advanced + correction
            moved = shifted(advanced, "tm", 1)
            return jnp.where(slice_index == 0, anchor, moved)

        return lax.fori_loop(0, slice_count - 1, one_round, anchor)

    def fine_sweep(fields):
        deflect, velocity = (fields[0], fields[1])
        first_row = tile_index * tile_rows
        for substep in range(fine_steps):
            padded = extended(deflect, (("span", 0),), 2)
            loading = point_loads(
                axle_rows[substep],
                axle_cols[substep],
                weights[substep],
                first_row,
                tile_rows,
                width,
            )
            deflect, velocity = advance(
                padded, deflect, velocity, column_stiff, loading, 1.0, TIME_STEP
            )
        return jnp.stack([deflect, velocity])

    anchor = restrict(start_state)
    first_chain = relay(anchor, None)
    first_old = coarse_step(first_chain, own_loading)
    start_zero = jnp.where(slice_index == 0, start_state, prolong(first_chain))
    sweep_zero = fine_sweep(start_zero)
    second_chain = relay(anchor, restrict(sweep_zero) - first_old)
    second_old = coarse_step(second_chain, own_loading)
    prior = shifted(sweep_zero, "tm", 1)
    start_one = jnp.where(
        slice_index == 0, start_state, prior + prolong(second_chain - restrict(prior))
    )
    sweep_one = fine_sweep(start_one)
    third_correction = restrict(sweep_one) - second_old
    third_chain = relay(anchor, third_correction)
    following = coarse_step(third_chain, own_loading) + third_correction
    end_state = sweep_one + prolong(following - restrict(sweep_one))
    return end_state[None]


SLICES = 4
LANES = 128
GROUPS = 8
MARGIN = 8
REACH = 48
CREACH = REACH // 4
KEPT = 24
RATIO = TIME_STEP * TIME_STEP


def lane_index(rows):
    return lax.broadcasted_iota(jnp.int32, (rows, LANES), 1)


def from_left(x):
    lane = lane_index(x.shape[0])
    source = jnp.where(lane < 8, (lane + 119) % LANES, lane - 8)
    moved = jnp.take_along_axis(x, source, axis=1, mode="promise_in_bounds")
    return jnp.where(lane == 0, 0.0, moved)


def from_right(x):
    lane = lane_index(x.shape[0])
    source = jnp.where(lane >= 120, (lane + 9) % LANES, lane + 8)
    moved = jnp.take_along_axis(x, source, axis=1, mode="promise_in_bounds")
    return jnp.where(lane == LANES - 1, 0.0, moved)


def interleave(pieces):
    pieces = list(pieces)
    lane = lane_index(pieces[0].shape[0])
    for dist in (1, 2, 4):
        keep = (lane & dist) == 0
        for low in range(GROUPS):
            if low & dist:
                continue
            high = low + dist
            first, second = pieces[low], pieces[high]
            pieces[low] = jnp.where(keep, first, pltpu.roll(second, dist, 1))
            pieces[high] = jnp.where(keep, pltpu.roll(first, LANES - dist, 1), second)
    return pieces


def tall(row_vreg, rows):
    return jnp.concatenate([row_vreg] * (rows // 8), axis=0)


class Plan:
    def __init__(self, tile_rows, span, steps, axles):
        self.tile = tile_rows
        self.rows = tile_rows + 2 * REACH
        self.buf = self.rows + 2 * MARGIN
        self.crows = self.rows // 4
        self.cbuf = self.crows + 2 * MARGIN
        self.span = span
        self.steps = steps
        self.axles = axles
        self.coarse_tau = TIME_STEP * steps

    def stiffness(self, classes_ref, table_ref, coef, ccoef):
        entries = table_ref.shape[0]
        pieces = []
        for q in range(GROUPS):
            cls = jnp.broadcast_to(classes_ref[:, q * LANES : (q + 1) * LANES], (8, LANES))
            value = jnp.zeros((8, LANES), jnp.float32)
            for entry in range(entries):
                value = jnp.where(cls == entry, table_ref[entry], value)
            pieces.append(value)
        stiff = interleave(pieces)
        for a in range(GROUPS):
            s = stiff[a]
            coef[0, a] = (2.0 - TIME_STEP * DAMPING) - RATIO * (6.0 * s + 10.0)
            coef[1, a] = RATIO * (4.0 * s + 2.0)
            coef[2, a] = -RATIO * s
        for g in range(2):
            ccoef[g] = 0.25 * (stiff[4 * g] + stiff[4 * g + 1] + stiff[4 * g + 2] + stiff[4 * g + 3])

    def clear_outside(self, ref, tile_index):
        for outside, first in (
            (tile_index == 0, MARGIN + REACH - 8),
            (tile_index == self.span - 1, MARGIN + REACH + self.tile),
        ):
            for a in range(GROUPS):
                rows = pl.ds(first, 8)
                ref[a, rows, :] = jnp.where(outside, 0.0, ref[a, rows, :])

    def block(self, src, dst, coef, r0, size):
        def at(a, offset):
            return src[a, pl.ds(r0 + offset, size), :]

        w, s1, t = {}, {}, {}

        def make(a):
            w[a] = at(a, 0)
            s1[a] = at(a, -1) + at(a, 1)
            t[a] = s1[a] - 6.0 * w[a]

        for a in (6, 7, 0, 1):
            make(a)
        w[-2], w[-1], t[-1] = from_left(w[6]), from_left(w[7]), from_left(t[7])
        w[8], w[9], t[8] = from_right(w[0]), from_right(w[1]), from_right(t[0])
        for a in range(GROUPS):
            if a + 2 not in w:
                make(a + 2)
            s2 = at(a, -2) + at(a, 2)
            across = (t[a - 1] + t[a + 1]) + (w[a - 2] + w[a + 2])
            along = tall(coef[2, a], size) * s2 + tall(coef[1, a], size) * s1[a]
            along = along + tall(coef[0, a], size) * w[a]
            old = dst[a, pl.ds(r0, size), :]
            dst[a, pl.ds(r0, size), :] = along - RATIO * across - (1.0 - TIME_STEP * DAMPING) * old

    def axle(self, ax, loads, number, step, i):
        base = (number * self.steps + step) * LANES + i
        return ax[base], ax[base + self.axles], loads[ax[base + 2 * self.axles]]

    def sweep(self, cur, prev, coef, ax, loads, number, wanted, tile_index):
        origin = tile_index * self.tile - REACH

        def advance_once(src, dst, step, around):
            lane = lane_index(1)
            for i in range(self.axles):
                row, col, weight = self.axle(ax, loads, number, step, i)
                local = row - origin
                inside = jnp.logical_and(local >= 0, local < self.rows)
                force = jnp.where(inside, weight * (-RATIO / (1.0 - TIME_STEP * DAMPING)), 0.0)
                place = jnp.where(inside, local, 0) + MARGIN
                where = ((col >> 3) & 15) * 8 + (col >> 7)
                group = col & 7
                here = dst[group, pl.ds(place, 1), :]
                dst[group, pl.ds(place, 1), :] = here + jnp.where(lane == where, force, 0.0)
            half = self.tile // 2 + around
            for first in (MARGIN + REACH - around, MARGIN + REACH - around + half):
                self.block(src, dst, coef, first, half)
            self.clear_outside(dst, tile_index)

        for first in range(0, self.steps, 4):
            around = wanted + 2 * (self.steps - first)

            def two(half, carry):
                advance_once(cur, prev, 2 * half, around)
                advance_once(prev, cur, 2 * half + 1, around)
                return carry

            lax.fori_loop(first // 2, first // 2 + 2, two, 0)

    def state_copies(self, state, cur, prev, sems, out):
        place = pl.ds(MARGIN + REACH - KEPT, self.tile + 2 * KEPT)
        copies = []
        for f, ref in enumerate((cur, prev)):
            ends = (ref.at[:, place, :], state.at[f])
            copies.append(pltpu.make_async_copy(*(ends if out else ends[::-1]), sems.at[f]))
        return copies

    def inside(self, tile_index):
        row = lax.broadcasted_iota(jnp.int32, (self.crows, LANES), 0)
        row = row + (tile_index * (self.tile // 4) - CREACH)
        return jnp.logical_and(row >= 0, row < self.span * (self.tile // 4))

    def restricted(self, cur, prev, tile_index):
        keep = self.inside(tile_index)
        fields = []
        for ref in (cur, prev):
            halves = []
            for g in range(2):
                total = None
                for a in range(4 * g, 4 * g + 4):
                    for j in range(4):
                        piece = ref[a, pl.ds(MARGIN + j, self.crows, stride=4), :]
                        total = piece if total is None else total + piece
                halves.append(jnp.where(keep, total * 0.0625, 0.0))
            fields.append(halves)
        now, before = fields
        return now, [now[g] - before[g] for g in range(2)]

    def add_prolonged(self, cur, prev, field, fresh):
        now, change = field
        for g in range(2):
            before = now[g] - change[g]
            for a in range(4 * g, 4 * g + 4):
                for j in range(4):
                    place = pl.ds(MARGIN + j, self.crows, stride=4)
                    if fresh:
                        cur[a, place, :] = now[g]
                        prev[a, place, :] = before
                    else:
                        cur[a, place, :] = cur[a, place, :] + now[g]
                        prev[a, place, :] = prev[a, place, :] + before

    def coarse_loads(self, cload, ax, loads, number, tile_index):
        origin = tile_index * (self.tile // 4) - CREACH
        for g in range(2):
            cload[g] = jnp.zeros((self.cbuf, LANES), jnp.float32)
        lane = lane_index(1)
        scale = TIME_STEP * self.coarse_tau / (16.0 * self.steps)

        def one_step(step, carry):
            for i in range(self.axles):
                row, col, weight = self.axle(ax, loads, number, step, i)
                local = (row >> 2) - origin
                inside = jnp.logical_and(local >= 0, local < self.crows)
                force = jnp.where(inside, scale * weight, 0.0)
                place = jnp.where(inside, local, 0) + MARGIN
                where = ((col >> 3) & 15) * 8 + (col >> 7)
                group = (col >> 2) & 1
                here = cload[group, pl.ds(place, 1), :]
                cload[group, pl.ds(place, 1), :] = here + jnp.where(lane == where, force, 0.0)
            return carry

        lax.fori_loop(0, self.steps, one_step, 0)

    def coarse(self, field, cwork, ccoef, tile_index, cload=None):
        now, change = field
        rows = self.crows
        for g in range(2):
            cwork[g, pl.ds(MARGIN, rows), :] = now[g]

        def at(g, offset):
            return cwork[g, pl.ds(MARGIN + offset, rows), :]

        keep = self.inside(tile_index)
        w = now
        s1 = [at(g, -1) + at(g, 1) for g in range(2)]
        s2 = [at(g, -2) + at(g, 2) for g in range(2)]
        t = [s1[g] - 6.0 * w[g] for g in range(2)]
        left, right = [from_left(t[1]), t[0]], [t[1], from_right(t[0])]
        kappa = TIME_STEP * self.coarse_tau / COARSE_SPACING
        grown, moved = [], []
        for g in range(2):
            s = tall(ccoef[g], rows)
            across = (left[g] + right[g]) + (from_left(w[g]) + from_right(w[g]))
            stiff = across + s * s2[g] - (4.0 * s + 2.0) * s1[g] + (6.0 * s + 10.0) * w[g]
            value = (1.0 - self.coarse_tau * DAMPING) * change[g] - kappa * stiff
            if cload is not None:
                value = value + cload[g, pl.ds(MARGIN, rows), :]
            value = jnp.where(keep, value, 0.0)
            moved.append(value)
            grown.append(w[g] + (self.coarse_tau / TIME_STEP) * value)
        return grown, moved


def put(ref, slot, field):
    for f in range(2):
        for g in range(2):
            ref[slot, f, g] = field[f][g]


def get(ref, slot):
    return [[ref[slot, f, g] for g in range(2)] for f in range(2)]


def plus(x, y):
    return [[x[f][g] + y[f][g] for g in range(2)] for f in range(2)]


def minus(x, y):
    return [[x[f][g] - y[f][g] for g in range(2)] for f in range(2)]


def load_rows(ref, cur, prev, offset, count):
    half = count // 2

    def one(j, carry):
        r = pl.multiple_of(j * half, 8)
        fields = []
        for f in range(2):
            fields.append(interleave(
                [ref[f, pl.ds(r, half), q * LANES : (q + 1) * LANES] for q in range(GROUPS)]))
        place = pl.multiple_of(offset + r, 8)
        for a in range(GROUPS):
            cur[a, pl.ds(place, half), :] = fields[0][a]
            prev[a, pl.ds(place, half), :] = fields[0][a] - TIME_STEP * fields[1][a]
        return carry

    lax.fori_loop(0, 2, one, 0)


def own_kernel(plan):
    def body(table, loads, classes, axle_rows, axle_cols, axle_class, start, own, coef, ccoef, packed,
             loads_out):
        packed[...] = jnp.zeros(packed.shape, jnp.int32)
        for field, ref in enumerate((axle_rows, axle_cols, axle_class)):
            packed[:, field * plan.axles : (field + 1) * plan.axles] = ref[...]
        for entry in range(loads.shape[0]):
            loads_out[entry] = loads[entry]
        plan.stiffness(classes, table, coef, ccoef)
        load_rows(start, own.at[0], own.at[1], 0, plan.tile)

    return body


def arrival_kernel(plan):
    def body(meta, ax, loads, mine, near, cload):
        load_rows(mine, near.at[0], near.at[1], 0, REACH)
        for number in range(2):
            plan.coarse_loads(cload.at[number], ax, loads, number, meta[1])

    return body


def first_kernel(plan):
    def body(meta, ax, loads, coef, ccoef, own, near, other, cload, state, send, keep, cwork, cur, prev,
             sems):
        number, tile_index = meta[0], meta[1]
        for g in range(2):
            cwork[g] = jnp.zeros((plan.cbuf, LANES), jnp.float32)
        even = ((tile_index + number) & 1) == 0
        below = MARGIN + REACH + plan.tile
        near_first = pl.multiple_of(jnp.where(even, below, MARGIN), 8)
        for f, ref in enumerate((cur, prev)):
            for a in range(GROUPS):
                ref[a, pl.ds(0, MARGIN), :] = jnp.zeros((MARGIN, LANES), jnp.float32)
                ref[a, pl.ds(MARGIN + plan.rows, MARGIN), :] = jnp.zeros((MARGIN, LANES), jnp.float32)
                ref[a, pl.ds(MARGIN + REACH, plan.tile), :] = own[f, a]
                ref[a, pl.ds(near_first, REACH), :] = near[f, a]
        load_rows(other, cur, prev, jnp.where(even, MARGIN, below), REACH)
        plan.clear_outside(cur, tile_index)
        plan.clear_outside(prev, tile_index)
        send[...] = jnp.zeros(send.shape, jnp.float32)

        def sweep(slice_number, wanted):
            plan.sweep(cur, prev, coef, ax, loads, slice_number, wanted, tile_index)

        @pl.when(number >= 2)
        def _():
            put(keep, 0, plan.restricted(cur, prev, tile_index))

        sweep(0, 32)

        @pl.when(number >= 2)
        def _():
            chain = plan.coarse(get(keep, 0), cwork, ccoef, tile_index, cload.at[0])
            put(keep, 0, chain)
            gap = minus(plan.restricted(cur, prev, tile_index), chain)
            put(keep, 1, plan.coarse(gap, cwork, ccoef, tile_index))

        @pl.when(number == 3)
        def _():
            put(keep, 0, plan.coarse(get(keep, 0), cwork, ccoef, tile_index, cload.at[1]))

        @pl.when((number & 1) == 1)
        def _():
            sweep(1, 16)

        @pl.when(number == 3)
        def _():
            restricted = plan.restricted(cur, prev, tile_index)
            put(send, 0, restricted)
            put(keep, 2, restricted)

        @pl.when(number == 3)
        def _():
            plan.add_prolonged(cur, prev, get(keep, 0), True)
            sweep(2, 16)
            put(keep, 3, plan.restricted(cur, prev, tile_index))

        @pl.when(number == 2)
        def _():
            plan.add_prolonged(cur, prev, get(keep, 0), True)
            sweep(1, 24)
            restricted = plan.restricted(cur, prev, tile_index)
            put(send, 0, restricted)
            correction = get(keep, 1)
            put(keep, 3, plus(restricted, correction))
            plan.add_prolonged(cur, prev, correction, False)
            sweep(2, 8)
            put(send, 1, plan.restricted(cur, prev, tile_index))

        copies = plan.state_copies(state, cur, prev, sems, True)
        for copy in copies:
            copy.start()
        for copy in copies:
            copy.wait()

    return body


def second_kernel(plan):
    def body(meta, ax, loads, coef, ccoef, state, keep, got, out, cwork, cur, prev, corr, sems):
        number, tile_index = meta[0], meta[1]
        copies = plan.state_copies(state, cur, prev, sems, False)
        for copy in copies:
            copy.start()
        for g in range(2):
            cwork[g] = jnp.zeros((plan.cbuf, LANES), jnp.float32)
        for copy in copies:
            copy.wait()

        @pl.when(number == 2)
        def _():
            gap = minus(get(got, 0), get(keep, 3))
            put(corr, 0, plan.coarse(gap, cwork, ccoef, tile_index))

        @pl.when(number == 3)
        def _():
            second = plus(get(got, 0), get(keep, 1))
            third = plan.coarse(minus(second, get(keep, 0)), cwork, ccoef, tile_index)
            plan.add_prolonged(cur, prev, third, False)
            plan.sweep(cur, prev, coef, ax, loads, 3, 0, tile_index)
            early = plan.coarse(minus(get(keep, 2), second), cwork, ccoef, tile_index)
            gap = minus(plus(early, get(got, 1)), plus(get(keep, 3), third))
            put(corr, 0, plan.coarse(gap, cwork, ccoef, tile_index))

        @pl.when(number >= 2)
        def _():
            plan.add_prolonged(cur, prev, get(corr, 0), False)

        def one(j, carry):
            r = pl.multiple_of(j * 32, 32)
            place = pl.multiple_of(MARGIN + REACH + r, 8)
            now = [cur[a, pl.ds(place, 32), :] for a in range(GROUPS)]
            speed = [(now[a] - prev[a, pl.ds(place, 32), :]) * (1.0 / TIME_STEP) for a in range(GROUPS)]
            for f, pieces in enumerate((interleave(now), interleave(speed))):
                for q in range(GROUPS):
                    out[0, f, pl.ds(r, 32), q * LANES : (q + 1) * LANES] = pieces[q]
            return carry

        lax.fori_loop(0, plan.tile // 32, one, 0)

    return body


def paired_plan(mesh):
    slices, tiles = mesh.shape["tm"], mesh.shape["span"]

    def joint(slice_number, tile_index):
        return slice_number * tiles + tile_index

    halos = []
    for k in range(slices):
        for s in range(tiles):
            partner = s + 1 if (s + k) % 2 == 0 else s - 1
            target = joint(k, partner) if 0 <= partner < tiles else joint(k ^ 2, s)
            halos.append((joint(k, s), target))
    swap = [(k, k ^ 1) for k in range(slices)]
    smem = pl.BlockSpec(memory_space=pltpu.SMEM)
    vmem = pl.BlockSpec(memory_space=pltpu.VMEM)
    hbm = pl.BlockSpec(memory_space=pl.ANY)
    params = pltpu.CompilerParams(vmem_limit_bytes=40 * 2**20)

    def on_pair(start_state, stiff_class, class_stiffness, axle_rows, axle_cols, axle_class, load_table):
        tile_rows = start_state.shape[1]
        steps, axles = axle_rows.shape
        plan = Plan(tile_rows, tiles, steps, axles)
        number = lax.axis_index("tm")
        tile_index = lax.axis_index("span")
        even = ((tile_index + number) & 1) == 0
        edge = lax.dynamic_slice_in_dim(
            start_state, jnp.where(even, tile_rows - REACH, 0), REACH, axis=1)
        mine = lax.ppermute(edge, ("tm", "span"), halos)
        f32 = jnp.float32
        classes = stiff_class.reshape(1, -1)

        def shape(*dims):
            return jax.ShapeDtypeStruct(dims, f32)

        own, coef, ccoef, packed, loads = pl.pallas_call(
            own_kernel(plan),
            out_shape=(
                shape(2, GROUPS, tile_rows, LANES),
                shape(3, GROUPS, 8, LANES),
                shape(2, 8, LANES),
                jax.ShapeDtypeStruct((steps, LANES), jnp.int32),
                shape(*load_table.shape),
            ),
            in_specs=[smem, smem] + [vmem] * 5,
            out_specs=(vmem, vmem, vmem, vmem, smem),
            compiler_params=params,
        )(class_stiffness, load_table, classes, axle_rows, axle_cols, axle_class, start_state)
        ax = lax.all_gather(packed, "tm").reshape(-1)
        mine, ax = lax.optimization_barrier((mine, ax))
        other = lax.ppermute(mine, "tm", swap)
        meta = jnp.stack([number, tile_index]).astype(jnp.int32)
        coarse = (2, 2, plan.crows, LANES)
        frame = [
            pltpu.VMEM((2, plan.cbuf, LANES), f32),
            pltpu.VMEM((GROUPS, plan.buf, LANES), f32),
            pltpu.VMEM((GROUPS, plan.buf, LANES), f32),
        ]

        near, cload = pl.pallas_call(
            arrival_kernel(plan),
            out_shape=(shape(2, GROUPS, REACH, LANES), shape(2, 2, plan.cbuf, LANES)),
            in_specs=[smem, smem, smem, vmem],
            out_specs=(vmem, vmem),
            compiler_params=params,
        )(meta, ax, loads, mine)
        state, send, keep = pl.pallas_call(
            first_kernel(plan),
            out_shape=(shape(2, GROUPS, tile_rows + 2 * KEPT, LANES), shape(2, *coarse), shape(4, *coarse)),
            in_specs=[smem] * 3 + [vmem] * 6,
            out_specs=(hbm, vmem, vmem),
            scratch_shapes=frame + [pltpu.SemaphoreType.DMA((2,))],
            compiler_params=params,
        )(meta, ax, loads, coef, ccoef, own, near, other, cload)
        got = lax.ppermute(send, "tm", swap)
        return pl.pallas_call(
            second_kernel(plan),
            out_shape=shape(1, *start_state.shape),
            in_specs=[smem] * 3 + [vmem, vmem, hbm, vmem, vmem],
            out_specs=vmem,
            scratch_shapes=frame + [pltpu.VMEM((1,) + coarse, f32), pltpu.SemaphoreType.DMA((2,))],
            compiler_params=params,
        )(meta, ax, loads, coef, ccoef, state, keep, got)

    return on_pair


def solution(mesh):
    in_specs = (
        P(None, ("parts", "span"), None),
        P("parts"),
        P(),
        P(("parts", "tm"), None),
        P(("parts", "tm"), None),
        P(("parts", "tm"), None),
        P(),
    )
    out_specs = P("tm", None, ("parts", "span"), None)
    body = paired_plan(mesh) if mesh.shape["tm"] == SLICES else on_device
    return jax.shard_map(body, mesh=mesh, in_specs=in_specs, out_specs=out_specs, check_vma=False)
```

```python
import jax
import jax.numpy as jnp
from jax import lax
from jax.experimental import pallas as pl
from jax.experimental.pallas import tpu as pltpu
from jax.sharding import PartitionSpec as P

TIME_STEP = 0.2
DAMPING = 0.05
TWIST = 0.5
CROSS_STIFF = 1.0
COARSE_SPACING = 256.0


def extended(cells, sides, width):
    for axis, dim in sides:
        count = lax.axis_size(axis)
        ends = count - 1
        head = lax.slice_in_dim(cells, 0, width, axis=dim)
        tail = lax.slice_in_dim(cells, cells.shape[dim] - width, cells.shape[dim], axis=dim)
        cells = jnp.concatenate(
            [
                lax.ppermute(tail, axis, [(i, (i + 1) % count) for i in range(ends)]),
                cells,
                lax.ppermute(head, axis, [((i + 1) % count, i) for i in range(ends)]),
            ],
            axis=dim,
        )
    return cells


def shifted(value, axis, steps):
    count = lax.axis_size(axis)
    leading, last = (max(0, -steps), min(count, count - steps))
    return lax.ppermute(value, axis, [(source, source + steps) for source in range(leading, last)])


def stiffness_term(padded, column_stiff):
    widened = jnp.pad(padded, ((0, 0), (2, 2)))
    along_rows = widened[2:] - 2.0 * widened[1:-1] + widened[:-2]
    along_four = along_rows[2:] - 2.0 * along_rows[1:-1] + along_rows[:-2]
    across = widened[:, 2:] - 2.0 * widened[:, 1:-1] + widened[:, :-2]
    across_four = across[:, 2:] - 2.0 * across[:, 1:-1] + across[:, :-2]
    mixed_term = across[2:] - 2.0 * across[1:-1] + across[:-2]
    return (
        column_stiff * along_four[:, 2:-2]
        + 2.0 * TWIST * mixed_term[1:-1, 1:-1]
        + CROSS_STIFF * across_four[2:-2]
    )


def advance(padded, deflect, velocity, column_stiff, loading, spacing, time_step):
    velocity = (1.0 - time_step * DAMPING) * velocity + time_step * (
        loading - stiffness_term(padded, column_stiff) / spacing
    )
    return (deflect + time_step * velocity, velocity)


def restrict(fine_field):
    leading = fine_field.shape[:-2]
    row_count = fine_field.shape[-2]
    col_count = fine_field.shape[-1]
    return jnp.mean(
        fine_field.reshape(leading + (row_count // 4, 4, col_count // 4, 4)), axis=(-3, -1)
    )


def prolong(coarse):
    return jnp.repeat(jnp.repeat(coarse, 4, axis=-2), 4, axis=-1)


def table_lookup(indices, table):
    entries = table.shape[0]
    matches = indices[..., None] == lax.iota(jnp.int32, entries)
    return jnp.sum(jnp.where(matches, table, 0.0), axis=-1)


def point_loads(axle_row, axle_col, weights, first_row, row_total, col_total):
    row_hot = jnp.where(
        axle_row[:, None] - first_row == lax.iota(jnp.int32, row_total)[None, :],
        weights[:, None],
        0.0,
    )
    col_hot = jnp.where(axle_col[:, None] == lax.iota(jnp.int32, col_total)[None, :], 1.0, 0.0)
    return jnp.einsum(
        "ar,ac->rc",
        row_hot,
        col_hot,
        precision=lax.Precision.HIGHEST,
        preferred_element_type=jnp.float32,
    )


def coarse_loading(step_rows, step_cols, weights, first_row, coarse_count, coarse_cols):
    step_total = step_rows.shape[0]
    scaled = weights.reshape(-1) / (16.0 * step_total)
    return point_loads(
        step_rows.reshape(-1) // 4,
        step_cols.reshape(-1) // 4,
        scaled,
        first_row,
        coarse_count,
        coarse_cols,
    )


def on_device(
    start_state, stiff_class, class_stiffness, axle_rows, axle_cols, axle_class, load_table
):
    slice_count = lax.axis_size("tm")
    tile_index = lax.axis_index("span")
    slice_index = lax.axis_index("tm")
    tile_rows = start_state.shape[1]
    width = start_state.shape[2]
    coarse_cols = width // 4
    fine_steps = axle_rows.shape[0]
    coarse_first = tile_index * (tile_rows // 4)
    coarse_count = tile_rows // 4
    column_stiff = table_lookup(stiff_class, class_stiffness)
    coarse_stiff = jnp.mean(column_stiff.reshape(coarse_cols, 4), axis=-1)
    weights = table_lookup(axle_class, load_table)
    own_loading = coarse_loading(
        axle_rows, axle_cols, weights, coarse_first, coarse_count, coarse_cols
    )
    coarse_tau = TIME_STEP * fine_steps

    def coarse_step(fields, loading):
        padded = extended(fields[0], (("span", 0),), 2)
        deflect, velocity = advance(
            padded, fields[0], fields[1], coarse_stiff, loading, COARSE_SPACING, coarse_tau
        )
        return jnp.stack([deflect, velocity])

    def relay(anchor, correction):

        def one_round(round_index, current):
            advanced = coarse_step(current, own_loading)
            if correction is not None:
                advanced = advanced + correction
            moved = shifted(advanced, "tm", 1)
            return jnp.where(slice_index == 0, anchor, moved)

        return lax.fori_loop(0, slice_count - 1, one_round, anchor)

    def fine_sweep(fields):
        deflect, velocity = (fields[0], fields[1])
        first_row = tile_index * tile_rows
        for substep in range(fine_steps):
            padded = extended(deflect, (("span", 0),), 2)
            loading = point_loads(
                axle_rows[substep],
                axle_cols[substep],
                weights[substep],
                first_row,
                tile_rows,
                width,
            )
            deflect, velocity = advance(
                padded, deflect, velocity, column_stiff, loading, 1.0, TIME_STEP
            )
        return jnp.stack([deflect, velocity])

    anchor = restrict(start_state)
    first_chain = relay(anchor, None)
    first_old = coarse_step(first_chain, own_loading)
    start_zero = jnp.where(slice_index == 0, start_state, prolong(first_chain))
    sweep_zero = fine_sweep(start_zero)
    second_chain = relay(anchor, restrict(sweep_zero) - first_old)
    second_old = coarse_step(second_chain, own_loading)
    prior = shifted(sweep_zero, "tm", 1)
    start_one = jnp.where(
        slice_index == 0, start_state, prior + prolong(second_chain - restrict(prior))
    )
    sweep_one = fine_sweep(start_one)
    third_correction = restrict(sweep_one) - second_old
    third_chain = relay(anchor, third_correction)
    following = coarse_step(third_chain, own_loading) + third_correction
    end_state = sweep_one + prolong(following - restrict(sweep_one))
    return end_state[None]


SLICES = 4
LANES = 128
GROUPS = 8
MARGIN = 8
REACH = 48
CREACH = REACH // 4
KEPT = 24
RATIO = TIME_STEP * TIME_STEP
DECAY = 1.0 - TIME_STEP * DAMPING
ROOT = DECAY**0.5


def lane_index(rows):
    return lax.broadcasted_iota(jnp.int32, (rows, LANES), 1)


def from_left(x):
    lane = lane_index(x.shape[0])
    source = jnp.where(lane < 8, (lane + 119) % LANES, lane - 8)
    moved = jnp.take_along_axis(x, source, axis=1, mode="promise_in_bounds")
    return jnp.where(lane == 0, 0.0, moved)


def from_right(x):
    lane = lane_index(x.shape[0])
    source = jnp.where(lane >= 120, (lane + 9) % LANES, lane + 8)
    moved = jnp.take_along_axis(x, source, axis=1, mode="promise_in_bounds")
    return jnp.where(lane == LANES - 1, 0.0, moved)


def interleave(pieces):
    pieces = list(pieces)
    lane = lane_index(pieces[0].shape[0])
    for dist in (1, 2, 4):
        keep = (lane & dist) == 0
        for low in range(GROUPS):
            if low & dist:
                continue
            high = low + dist
            first, second = pieces[low], pieces[high]
            pieces[low] = jnp.where(keep, first, pltpu.roll(second, dist, 1))
            pieces[high] = jnp.where(keep, pltpu.roll(first, LANES - dist, 1), second)
    return pieces


def tall(row_vreg, rows):
    return jnp.concatenate([row_vreg] * (rows // 8), axis=0)


class Plan:
    def __init__(self, tile_rows, span, steps, axles):
        self.tile = tile_rows
        self.rows = tile_rows + 2 * REACH
        self.buf = self.rows + 2 * MARGIN
        self.crows = self.rows // 4
        self.cbuf = self.crows + 2 * MARGIN
        self.span = span
        self.steps = steps
        self.axles = axles
        self.coarse_tau = TIME_STEP * steps
        self.grown = DECAY ** (-0.5 * steps)

    def stiffness(self, classes_ref, table_ref, coef, ccoef):
        entries = table_ref.shape[0]
        pieces = []
        for q in range(GROUPS):
            cls = jnp.broadcast_to(classes_ref[:, q * LANES : (q + 1) * LANES], (8, LANES))
            value = jnp.zeros((8, LANES), jnp.float32)
            for entry in range(entries):
                value = jnp.where(cls == entry, table_ref[entry], value)
            pieces.append(value)
        stiff = interleave(pieces)
        for a in range(GROUPS):
            s = stiff[a]
            coef[0, a] = (1.0 + DECAY) / ROOT - (RATIO / ROOT) * (6.0 * s + 10.0)
            coef[1, a] = (RATIO / ROOT) * (4.0 * s + 2.0)
            coef[2, a] = (-RATIO / ROOT) * s
        for g in range(2):
            ccoef[g] = 0.25 * (stiff[4 * g] + stiff[4 * g + 1] + stiff[4 * g + 2] + stiff[4 * g + 3])

    def clear_outside(self, ref, tile_index):
        for outside, first in (
            (tile_index == 0, MARGIN + REACH - 8),
            (tile_index == self.span - 1, MARGIN + REACH + self.tile),
        ):
            for a in range(GROUPS):
                rows = pl.ds(first, 8)
                ref[a, rows, :] = jnp.where(outside, 0.0, ref[a, rows, :])

    def block(self, src, dst, coef, r0, size):
        def at(a, offset):
            return src[a, pl.ds(r0 + offset, size), :]

        w, s1, t = {}, {}, {}

        def make(a):
            w[a] = at(a, 0)
            s1[a] = at(a, -1) + at(a, 1)
            t[a] = s1[a] - 6.0 * w[a]

        for a in (6, 7, 0, 1):
            make(a)
        w[-2], w[-1], t[-1] = from_left(w[6]), from_left(w[7]), from_left(t[7])
        w[8], w[9], t[8] = from_right(w[0]), from_right(w[1]), from_right(t[0])
        for a in range(GROUPS):
            if a + 2 not in w:
                make(a + 2)
            s2 = at(a, -2) + at(a, 2)
            across = (t[a - 1] + t[a + 1]) + (w[a - 2] + w[a + 2])
            along = tall(coef[2, a], size) * s2 + tall(coef[1, a], size) * s1[a]
            along = along + tall(coef[0, a], size) * w[a]
            old = dst[a, pl.ds(r0, size), :]
            dst[a, pl.ds(r0, size), :] = along - (RATIO / ROOT) * across - old

    def axle(self, ax, loads, number, step, i):
        base = (number * self.steps + step) * LANES + i
        return ax[base], ax[base + self.axles], loads[ax[base + 2 * self.axles]]

    def sweep(self, cur, prev, coef, ax, loads, number, wanted, tile_index, grade):
        origin = tile_index * self.tile - REACH

        def advance_once(src, dst, step, around, scale):
            lane = lane_index(1)
            for i in range(self.axles):
                row, col, weight = self.axle(ax, loads, number, step, i)
                local = row - origin
                inside = jnp.logical_and(local >= 0, local < self.rows)
                force = jnp.where(inside, weight * (-RATIO * scale), 0.0)
                place = jnp.where(inside, local, 0) + MARGIN
                where = ((col >> 3) & 15) * 8 + (col >> 7)
                group = col & 7
                here = dst[group, pl.ds(place, 1), :]
                dst[group, pl.ds(place, 1), :] = here + jnp.where(lane == where, force, 0.0)
            half = self.tile // 2 + around
            for first in (MARGIN + REACH - around, MARGIN + REACH - around + half):
                self.block(src, dst, coef, first, half)
            self.clear_outside(dst, tile_index)

        for first in range(0, self.steps, 4):
            around = wanted + 2 * (self.steps - first)

            def two(half, scale):
                advance_once(cur, prev, 2 * half, around, scale)
                advance_once(prev, cur, 2 * half + 1, around, scale * (1.0 / ROOT))
                return scale * (1.0 / DECAY)

            start = jnp.float32(grade * DECAY ** (-0.5 * (first + 1)))
            lax.fori_loop(first // 2, first // 2 + 2, two, start)

    def state_copies(self, state, cur, prev, sems, out):
        place = pl.ds(MARGIN + REACH - KEPT, self.tile + 2 * KEPT)
        copies = []
        for f, ref in enumerate((cur, prev)):
            ends = (ref.at[:, place, :], state.at[f])
            copies.append(pltpu.make_async_copy(*(ends if out else ends[::-1]), sems.at[f]))
        return copies

    def inside(self, tile_index):
        row = lax.broadcasted_iota(jnp.int32, (self.crows, LANES), 0)
        row = row + (tile_index * (self.tile // 4) - CREACH)
        return jnp.logical_and(row >= 0, row < self.span * (self.tile // 4))

    def restricted(self, cur, prev, tile_index, grade):
        keep = self.inside(tile_index)
        fields = []
        for ref, scale in ((cur, 0.0625 / grade), (prev, 0.0625 / (grade * ROOT))):
            halves = []
            for g in range(2):
                total = None
                for a in range(4 * g, 4 * g + 4):
                    for j in range(4):
                        piece = ref[a, pl.ds(MARGIN + j, self.crows, stride=4), :]
                        total = piece if total is None else total + piece
                halves.append(jnp.where(keep, total * scale, 0.0))
            fields.append(halves)
        now, before = fields
        return now, [now[g] - before[g] for g in range(2)]

    def add_prolonged(self, cur, prev, field, fresh, grade, cut=0):
        count = self.crows - 2 * cut
        now = [value[cut : cut + count] for value in field[0]]
        change = [value[cut : cut + count] for value in field[1]]
        for g in range(2):
            before = (now[g] - change[g]) * (grade * ROOT)
            after = now[g] * grade
            for a in range(4 * g, 4 * g + 4):
                for j in range(4):
                    place = pl.ds(MARGIN + 4 * cut + j, count, stride=4)
                    if fresh:
                        cur[a, place, :] = after
                        prev[a, place, :] = before
                    else:
                        cur[a, place, :] = cur[a, place, :] + after
                        prev[a, place, :] = prev[a, place, :] + before

    def coarse_loads(self, cload, ax, loads, number, tile_index):
        origin = tile_index * (self.tile // 4) - CREACH
        lane = lane_index(1)
        scale = TIME_STEP * self.coarse_tau / (16.0 * self.steps)

        for step in range(self.steps):
            for i in range(self.axles):
                row, col, weight = self.axle(ax, loads, number, step, i)
                local = (row >> 2) - origin
                inside = jnp.logical_and(local >= 0, local < self.crows)
                force = jnp.where(inside, scale * weight, 0.0)
                place = jnp.where(inside, local, 0) + MARGIN
                where = ((col >> 3) & 15) * 8 + (col >> 7)
                group = (col >> 2) & 1
                here = cload[group, pl.ds(place, 1), :]
                cload[group, pl.ds(place, 1), :] = here + jnp.where(lane == where, force, 0.0)

    def coarse(self, field, cwork, ccoef, tile_index, cload=None):
        now, change = field
        rows = self.crows
        for g in range(2):
            cwork[g, pl.ds(MARGIN, rows), :] = now[g]

        def at(g, offset):
            return cwork[g, pl.ds(MARGIN + offset, rows), :]

        keep = self.inside(tile_index)
        w = now
        s1 = [at(g, -1) + at(g, 1) for g in range(2)]
        s2 = [at(g, -2) + at(g, 2) for g in range(2)]
        t = [s1[g] - 6.0 * w[g] for g in range(2)]
        left, right = [from_left(t[1]), t[0]], [t[1], from_right(t[0])]
        kappa = TIME_STEP * self.coarse_tau / COARSE_SPACING
        grown, moved = [], []
        for g in range(2):
            s = tall(ccoef[g], rows)
            across = (left[g] + right[g]) + (from_left(w[g]) + from_right(w[g]))
            stiff = across + s * s2[g] - (4.0 * s + 2.0) * s1[g] + (6.0 * s + 10.0) * w[g]
            value = (1.0 - self.coarse_tau * DAMPING) * change[g] - kappa * stiff
            if cload is not None:
                value = value + cload[g, pl.ds(MARGIN, rows), :]
            value = jnp.where(keep, value, 0.0)
            moved.append(value)
            grown.append(w[g] + (self.coarse_tau / TIME_STEP) * value)
        return grown, moved


def put(ref, slot, field):
    for f in range(2):
        for g in range(2):
            ref[slot, f, g] = field[f][g]


def get(ref, slot):
    return [[ref[slot, f, g] for g in range(2)] for f in range(2)]


def plus(x, y):
    return [[x[f][g] + y[f][g] for g in range(2)] for f in range(2)]


def minus(x, y):
    return [[x[f][g] - y[f][g] for g in range(2)] for f in range(2)]


def load_rows(ref, cur, prev, offset, count, beside=None):
    half = count // 2

    def one(j, carry):
        r = pl.multiple_of(j * half, 8)
        fields = []
        for f in range(2):
            fields.append(interleave(
                [ref[f, pl.ds(r, half), q * LANES : (q + 1) * LANES] for q in range(GROUPS)]))
        place = pl.multiple_of(offset + r, 8)
        for a in range(GROUPS):
            cur[a, pl.ds(place, half), :] = fields[0][a]
            prev[a, pl.ds(place, half), :] = ROOT * (fields[0][a] - TIME_STEP * fields[1][a])
        if beside is not None:
            beside(j)
        return carry

    lax.fori_loop(0, 2, one, 0)


def own_kernel(plan):
    def body(table, loads, classes, axle_rows, axle_cols, axle_class, start, own, coef, ccoef, packed,
             loads_out):
        packed[...] = jnp.zeros(packed.shape, jnp.int32)
        for field, ref in enumerate((axle_rows, axle_cols, axle_class)):
            packed[:, field * plan.axles : (field + 1) * plan.axles] = ref[...]
        for entry in range(loads.shape[0]):
            loads_out[entry] = loads[entry]
        plan.stiffness(classes, table, coef, ccoef)
        load_rows(start, own.at[0], own.at[1], 0, plan.tile)

    return body


def arrival_kernel(plan):
    def body(meta, ax, loads, mine, near, cload):
        cload[...] = jnp.zeros(cload.shape, jnp.float32)

        def beside(number):
            plan.coarse_loads(cload.at[number], ax, loads, number, meta[1])

        load_rows(mine, near.at[0], near.at[1], 0, REACH, beside)

    return body


def first_kernel(plan):
    def body(meta, ax, loads, coef, ccoef, own, near, other, cload, state, send, keep, cwork, cur, prev,
             sems):
        number, tile_index = meta[0], meta[1]
        for g in range(2):
            cwork[g] = jnp.zeros((plan.cbuf, LANES), jnp.float32)
        even = ((tile_index + number) & 1) == 0
        below = MARGIN + REACH + plan.tile
        near_first = pl.multiple_of(jnp.where(even, below, MARGIN), 8)
        for f, ref in enumerate((cur, prev)):
            for a in range(GROUPS):
                ref[a, pl.ds(0, MARGIN), :] = jnp.zeros((MARGIN, LANES), jnp.float32)
                ref[a, pl.ds(MARGIN + plan.rows, MARGIN), :] = jnp.zeros((MARGIN, LANES), jnp.float32)
                ref[a, pl.ds(MARGIN + REACH, plan.tile), :] = own[f, a]
                ref[a, pl.ds(near_first, REACH), :] = near[f, a]
        load_rows(other, cur, prev, jnp.where(even, MARGIN, below), REACH)
        plan.clear_outside(cur, tile_index)
        plan.clear_outside(prev, tile_index)
        send[...] = jnp.zeros(send.shape, jnp.float32)

        def sweep(slice_number, wanted, grade):
            plan.sweep(cur, prev, coef, ax, loads, slice_number, wanted, tile_index, grade)

        once, twice = plan.grown, plan.grown * plan.grown

        @pl.when(number >= 2)
        def _():
            put(keep, 0, plan.restricted(cur, prev, tile_index, 1.0))

        sweep(0, 32, 1.0)

        @pl.when(number >= 2)
        def _():
            chain = plan.coarse(get(keep, 0), cwork, ccoef, tile_index, cload.at[0])
            put(keep, 0, chain)
            gap = minus(plan.restricted(cur, prev, tile_index, once), chain)
            put(keep, 1, plan.coarse(gap, cwork, ccoef, tile_index))

        @pl.when(number == 3)
        def _():
            put(keep, 0, plan.coarse(get(keep, 0), cwork, ccoef, tile_index, cload.at[1]))

        @pl.when((number & 1) == 1)
        def _():
            sweep(1, 16, once)

        @pl.when(number == 3)
        def _():
            restricted = plan.restricted(cur, prev, tile_index, twice)
            put(send, 0, restricted)
            put(keep, 2, restricted)

        @pl.when(number == 3)
        def _():
            plan.add_prolonged(cur, prev, get(keep, 0), True, 1.0)
            sweep(2, 16, 1.0)
            put(keep, 3, plan.restricted(cur, prev, tile_index, once))

        @pl.when(number == 2)
        def _():
            plan.add_prolonged(cur, prev, get(keep, 0), True, 1.0)
            sweep(1, 24, 1.0)
            restricted = plan.restricted(cur, prev, tile_index, once)
            put(send, 0, restricted)
            correction = get(keep, 1)
            put(keep, 3, plus(restricted, correction))
            plan.add_prolonged(cur, prev, correction, False, once)
            sweep(2, 8, once)
            put(send, 1, plan.restricted(cur, prev, tile_index, twice))

        copies = plan.state_copies(state, cur, prev, sems, True)
        for copy in copies:
            copy.start()
        for copy in copies:
            copy.wait()

    return body


def second_kernel(plan):
    def body(meta, ax, loads, coef, ccoef, state, keep, got, out, cwork, cur, prev, corr, sems, ready):
        number, tile_index = meta[0], meta[1]
        copies = plan.state_copies(state, cur, prev, sems, False)
        for copy in copies:
            copy.start()
        for g in range(2):
            cwork[g] = jnp.zeros((plan.cbuf, LANES), jnp.float32)
        @pl.when(number == 2)
        def _():
            gap = minus(get(got, 0), get(keep, 3))
            put(corr, 0, plan.coarse(gap, cwork, ccoef, tile_index))

        @pl.when(number == 3)
        def _():
            second = plus(get(got, 0), get(keep, 1))
            third = plan.coarse(minus(second, get(keep, 0)), cwork, ccoef, tile_index)
            put(corr, 1, third)
            early = plan.coarse(minus(get(keep, 2), second), cwork, ccoef, tile_index)
            gap = minus(plus(early, get(got, 1)), plus(get(keep, 3), third))
            put(corr, 0, plan.coarse(gap, cwork, ccoef, tile_index))

        for copy in copies:
            copy.wait()

        @pl.when(number == 3)
        def _():
            plan.add_prolonged(cur, prev, get(corr, 1), False, plan.grown, 8)
            plan.sweep(cur, prev, coef, ax, loads, 3, 0, tile_index, plan.grown)

        @pl.when(number >= 2)
        def _():
            plan.add_prolonged(cur, prev, get(corr, 0), False, plan.grown * plan.grown, 8)

        back = jnp.where(number == 0, 1.0 / plan.grown, 1.0 / (plan.grown * plan.grown))
        parts = []
        size = plan.tile // 2
        for j in range(2):
            rows = pl.ds(j * size, size)
            place = pl.ds(MARGIN + REACH + j * size, size)
            now = [cur[a, place, :] * back for a in range(GROUPS)]
            speed = [(now[a] - prev[a, place, :] * (back * (1.0 / ROOT))) * (1.0 / TIME_STEP) for a in range(GROUPS)]
            for f, pieces in enumerate((interleave(now), interleave(speed))):
                for q in range(GROUPS):
                    ready[f, rows, q * LANES : (q + 1) * LANES] = pieces[q]
            parts.append(pltpu.make_async_copy(ready.at[:, rows, :], out.at[0, :, rows, :], sems.at[2 + j]))
            parts[j].start()
        for part in parts:
            part.wait()

    return body


def paired_plan(mesh):
    slices, tiles = mesh.shape["tm"], mesh.shape["span"]

    def joint(slice_number, tile_index):
        return slice_number * tiles + tile_index

    halos = []
    for k in range(slices):
        for s in range(tiles):
            partner = s + 1 if (s + k) % 2 == 0 else s - 1
            target = joint(k, partner) if 0 <= partner < tiles else joint(k ^ 2, s)
            halos.append((joint(k, s), target))
    swap = [(k, k ^ 1) for k in range(slices)]
    smem = pl.BlockSpec(memory_space=pltpu.SMEM)
    vmem = pl.BlockSpec(memory_space=pltpu.VMEM)
    hbm = pl.BlockSpec(memory_space=pl.ANY)
    params = pltpu.CompilerParams(vmem_limit_bytes=40 * 2**20)

    def on_pair(start_state, stiff_class, class_stiffness, axle_rows, axle_cols, axle_class, load_table):
        tile_rows = start_state.shape[1]
        steps, axles = axle_rows.shape
        plan = Plan(tile_rows, tiles, steps, axles)
        number = lax.axis_index("tm")
        tile_index = lax.axis_index("span")
        even = ((tile_index + number) & 1) == 0
        edge = lax.dynamic_slice_in_dim(
            start_state, jnp.where(even, tile_rows - REACH, 0), REACH, axis=1)
        mine = lax.ppermute(edge, ("tm", "span"), halos)
        f32 = jnp.float32
        classes = stiff_class.reshape(1, -1)

        def shape(*dims):
            return jax.ShapeDtypeStruct(dims, f32)

        own, coef, ccoef, packed, loads = pl.pallas_call(
            own_kernel(plan),
            out_shape=(
                shape(2, GROUPS, tile_rows, LANES),
                shape(3, GROUPS, 8, LANES),
                shape(2, 8, LANES),
                jax.ShapeDtypeStruct((steps, LANES), jnp.int32),
                shape(*load_table.shape),
            ),
            in_specs=[smem, smem] + [vmem] * 5,
            out_specs=(vmem, vmem, vmem, vmem, smem),
            compiler_params=params,
        )(class_stiffness, load_table, classes, axle_rows, axle_cols, axle_class, start_state)
        ax = lax.all_gather(packed, "tm").reshape(-1)
        mine, ax = lax.optimization_barrier((mine, ax))
        other = lax.ppermute(mine, "tm", swap)
        meta = jnp.stack([number, tile_index]).astype(jnp.int32)
        coarse = (2, 2, plan.crows, LANES)
        frame = [
            pltpu.VMEM((2, plan.cbuf, LANES), f32),
            pltpu.VMEM((GROUPS, plan.buf, LANES), f32),
            pltpu.VMEM((GROUPS, plan.buf, LANES), f32),
        ]

        near, cload = pl.pallas_call(
            arrival_kernel(plan),
            out_shape=(shape(2, GROUPS, REACH, LANES), shape(2, 2, plan.cbuf, LANES)),
            in_specs=[smem, smem, smem, vmem],
            out_specs=(vmem, vmem),
            compiler_params=params,
        )(meta, ax, loads, mine)
        state, send, keep = pl.pallas_call(
            first_kernel(plan),
            out_shape=(shape(2, GROUPS, tile_rows + 2 * KEPT, LANES), shape(2, *coarse), shape(4, *coarse)),
            in_specs=[smem] * 3 + [vmem] * 6,
            out_specs=(hbm, vmem, vmem),
            scratch_shapes=frame + [pltpu.SemaphoreType.DMA((2,))],
            compiler_params=params,
        )(meta, ax, loads, coef, ccoef, own, near, other, cload)
        got = lax.ppermute(send, "tm", swap)
        return pl.pallas_call(
            second_kernel(plan),
            out_shape=shape(1, *start_state.shape),
            in_specs=[smem] * 3 + [vmem, vmem, hbm, vmem, vmem],
            out_specs=hbm,
            scratch_shapes=frame
            + [pltpu.VMEM((2,) + coarse, f32), pltpu.SemaphoreType.DMA((4,))]
            + [pltpu.VMEM(start_state.shape, f32)],
            compiler_params=params,
        )(meta, ax, loads, coef, ccoef, state, keep, got)

    return on_pair


def solution(mesh):
    in_specs = (
        P(None, ("parts", "span"), None),
        P("parts"),
        P(),
        P(("parts", "tm"), None),
        P(("parts", "tm"), None),
        P(("parts", "tm"), None),
        P(),
    )
    out_specs = P("tm", None, ("parts", "span"), None)
    body = paired_plan(mesh) if mesh.shape["tm"] == SLICES else on_device
    return jax.shard_map(body, mesh=mesh, in_specs=in_specs, out_specs=out_specs, check_vma=False)
```

```python
import jax
import jax.numpy as jnp
from jax import lax
from jax.experimental import pallas as pl
from jax.experimental.pallas import tpu as pltpu
from jax.sharding import PartitionSpec as P

TIME_STEP = 0.2
DAMPING = 0.05
TWIST = 0.5
CROSS_STIFF = 1.0
COARSE_SPACING = 256.0


def extended(cells, sides, width):
    for axis, dim in sides:
        count = lax.axis_size(axis)
        ends = count - 1
        head = lax.slice_in_dim(cells, 0, width, axis=dim)
        tail = lax.slice_in_dim(cells, cells.shape[dim] - width, cells.shape[dim], axis=dim)
        cells = jnp.concatenate(
            [
                lax.ppermute(tail, axis, [(i, (i + 1) % count) for i in range(ends)]),
                cells,
                lax.ppermute(head, axis, [((i + 1) % count, i) for i in range(ends)]),
            ],
            axis=dim,
        )
    return cells


def shifted(value, axis, steps):
    count = lax.axis_size(axis)
    leading, last = (max(0, -steps), min(count, count - steps))
    return lax.ppermute(value, axis, [(source, source + steps) for source in range(leading, last)])


def stiffness_term(padded, column_stiff):
    widened = jnp.pad(padded, ((0, 0), (2, 2)))
    along_rows = widened[2:] - 2.0 * widened[1:-1] + widened[:-2]
    along_four = along_rows[2:] - 2.0 * along_rows[1:-1] + along_rows[:-2]
    across = widened[:, 2:] - 2.0 * widened[:, 1:-1] + widened[:, :-2]
    across_four = across[:, 2:] - 2.0 * across[:, 1:-1] + across[:, :-2]
    mixed_term = across[2:] - 2.0 * across[1:-1] + across[:-2]
    return (
        column_stiff * along_four[:, 2:-2]
        + 2.0 * TWIST * mixed_term[1:-1, 1:-1]
        + CROSS_STIFF * across_four[2:-2]
    )


def advance(padded, deflect, velocity, column_stiff, loading, spacing, time_step):
    velocity = (1.0 - time_step * DAMPING) * velocity + time_step * (
        loading - stiffness_term(padded, column_stiff) / spacing
    )
    return (deflect + time_step * velocity, velocity)


def restrict(fine_field):
    leading = fine_field.shape[:-2]
    row_count = fine_field.shape[-2]
    col_count = fine_field.shape[-1]
    return jnp.mean(
        fine_field.reshape(leading + (row_count // 4, 4, col_count // 4, 4)), axis=(-3, -1)
    )


def prolong(coarse):
    return jnp.repeat(jnp.repeat(coarse, 4, axis=-2), 4, axis=-1)


def table_lookup(indices, table):
    entries = table.shape[0]
    matches = indices[..., None] == lax.iota(jnp.int32, entries)
    return jnp.sum(jnp.where(matches, table, 0.0), axis=-1)


def point_loads(axle_row, axle_col, weights, first_row, row_total, col_total):
    row_hot = jnp.where(
        axle_row[:, None] - first_row == lax.iota(jnp.int32, row_total)[None, :],
        weights[:, None],
        0.0,
    )
    col_hot = jnp.where(axle_col[:, None] == lax.iota(jnp.int32, col_total)[None, :], 1.0, 0.0)
    return jnp.einsum(
        "ar,ac->rc",
        row_hot,
        col_hot,
        precision=lax.Precision.HIGHEST,
        preferred_element_type=jnp.float32,
    )


def coarse_loading(step_rows, step_cols, weights, first_row, coarse_count, coarse_cols):
    step_total = step_rows.shape[0]
    scaled = weights.reshape(-1) / (16.0 * step_total)
    return point_loads(
        step_rows.reshape(-1) // 4,
        step_cols.reshape(-1) // 4,
        scaled,
        first_row,
        coarse_count,
        coarse_cols,
    )


def on_device(
    start_state, stiff_class, class_stiffness, axle_rows, axle_cols, axle_class, load_table
):
    slice_count = lax.axis_size("tm")
    tile_index = lax.axis_index("span")
    slice_index = lax.axis_index("tm")
    tile_rows = start_state.shape[1]
    width = start_state.shape[2]
    coarse_cols = width // 4
    fine_steps = axle_rows.shape[0]
    coarse_first = tile_index * (tile_rows // 4)
    coarse_count = tile_rows // 4
    column_stiff = table_lookup(stiff_class, class_stiffness)
    coarse_stiff = jnp.mean(column_stiff.reshape(coarse_cols, 4), axis=-1)
    weights = table_lookup(axle_class, load_table)
    own_loading = coarse_loading(
        axle_rows, axle_cols, weights, coarse_first, coarse_count, coarse_cols
    )
    coarse_tau = TIME_STEP * fine_steps

    def coarse_step(fields, loading):
        padded = extended(fields[0], (("span", 0),), 2)
        deflect, velocity = advance(
            padded, fields[0], fields[1], coarse_stiff, loading, COARSE_SPACING, coarse_tau
        )
        return jnp.stack([deflect, velocity])

    def relay(anchor, correction):

        def one_round(round_index, current):
            advanced = coarse_step(current, own_loading)
            if correction is not None:
                advanced = advanced + correction
            moved = shifted(advanced, "tm", 1)
            return jnp.where(slice_index == 0, anchor, moved)

        return lax.fori_loop(0, slice_count - 1, one_round, anchor)

    def fine_sweep(fields):
        deflect, velocity = (fields[0], fields[1])
        first_row = tile_index * tile_rows
        for substep in range(fine_steps):
            padded = extended(deflect, (("span", 0),), 2)
            loading = point_loads(
                axle_rows[substep],
                axle_cols[substep],
                weights[substep],
                first_row,
                tile_rows,
                width,
            )
            deflect, velocity = advance(
                padded, deflect, velocity, column_stiff, loading, 1.0, TIME_STEP
            )
        return jnp.stack([deflect, velocity])

    anchor = restrict(start_state)
    first_chain = relay(anchor, None)
    first_old = coarse_step(first_chain, own_loading)
    start_zero = jnp.where(slice_index == 0, start_state, prolong(first_chain))
    sweep_zero = fine_sweep(start_zero)
    second_chain = relay(anchor, restrict(sweep_zero) - first_old)
    second_old = coarse_step(second_chain, own_loading)
    prior = shifted(sweep_zero, "tm", 1)
    start_one = jnp.where(
        slice_index == 0, start_state, prior + prolong(second_chain - restrict(prior))
    )
    sweep_one = fine_sweep(start_one)
    third_correction = restrict(sweep_one) - second_old
    third_chain = relay(anchor, third_correction)
    following = coarse_step(third_chain, own_loading) + third_correction
    end_state = sweep_one + prolong(following - restrict(sweep_one))
    return end_state[None]


SLICES = 4
LANES = 128
GROUPS = 8
MARGIN = 8
REACH = 48
CREACH = REACH // 4
KEPT = 24
RATIO = TIME_STEP * TIME_STEP
DECAY = 1.0 - TIME_STEP * DAMPING
ROOT = DECAY**0.5


def lane_index(rows):
    return lax.broadcasted_iota(jnp.int32, (rows, LANES), 1)


def from_left(x):
    lane = lane_index(x.shape[0])
    source = jnp.where(lane < 8, (lane + 119) % LANES, lane - 8)
    moved = jnp.take_along_axis(x, source, axis=1, mode="promise_in_bounds")
    return jnp.where(lane == 0, 0.0, moved)


def from_right(x):
    lane = lane_index(x.shape[0])
    source = jnp.where(lane >= 120, (lane + 9) % LANES, lane + 8)
    moved = jnp.take_along_axis(x, source, axis=1, mode="promise_in_bounds")
    return jnp.where(lane == LANES - 1, 0.0, moved)


def interleave(pieces):
    pieces = list(pieces)
    lane = lane_index(pieces[0].shape[0])
    for dist in (1, 2, 4):
        keep = (lane & dist) == 0
        for low in range(GROUPS):
            if low & dist:
                continue
            high = low + dist
            first, second = pieces[low], pieces[high]
            pieces[low] = jnp.where(keep, first, pltpu.roll(second, dist, 1))
            pieces[high] = jnp.where(keep, pltpu.roll(first, LANES - dist, 1), second)
    return pieces


def tall(row_vreg, rows):
    return jnp.concatenate([row_vreg] * (rows // 8), axis=0)


class Plan:
    def __init__(self, tile_rows, span, steps, axles):
        self.tile = tile_rows
        self.rows = tile_rows + 2 * REACH
        self.buf = self.rows + 2 * MARGIN
        self.crows = self.rows // 4
        self.cbuf = self.crows + 2 * MARGIN
        self.span = span
        self.steps = steps
        self.axles = axles
        self.coarse_tau = TIME_STEP * steps
        self.grown = DECAY ** (-0.5 * steps)

    def stiffness(self, classes_ref, table_ref, coef, ccoef):
        entries = table_ref.shape[0]
        pieces = []
        for q in range(GROUPS):
            cls = jnp.broadcast_to(classes_ref[:, q * LANES : (q + 1) * LANES], (8, LANES))
            value = jnp.zeros((8, LANES), jnp.float32)
            for entry in range(entries):
                value = jnp.where(cls == entry, table_ref[entry], value)
            pieces.append(value)
        stiff = interleave(pieces)
        for a in range(GROUPS):
            s = stiff[a]
            coef[0, a] = (1.0 + DECAY) / ROOT - (RATIO / ROOT) * (6.0 * s + 10.0)
            coef[1, a] = (RATIO / ROOT) * (4.0 * s + 2.0)
            coef[2, a] = (-RATIO / ROOT) * s
        for g in range(2):
            ccoef[g] = 0.25 * (stiff[4 * g] + stiff[4 * g + 1] + stiff[4 * g + 2] + stiff[4 * g + 3])

    def clear_outside(self, ref, tile_index):
        for outside, first in (
            (tile_index == 0, MARGIN + REACH - 8),
            (tile_index == self.span - 1, MARGIN + REACH + self.tile),
        ):
            for a in range(GROUPS):
                rows = pl.ds(first, 8)
                ref[a, rows, :] = jnp.where(outside, 0.0, ref[a, rows, :])

    def block(self, src, dst, coef, r0, size):
        def at(a, offset):
            return src[a, pl.ds(r0 + offset, size), :]

        w, s1, t = {}, {}, {}

        def make(a):
            w[a] = at(a, 0)
            s1[a] = at(a, -1) + at(a, 1)
            t[a] = s1[a] - 6.0 * w[a]

        for a in (6, 7, 0, 1):
            make(a)
        w[-2], w[-1], t[-1] = from_left(w[6]), from_left(w[7]), from_left(t[7])
        w[8], w[9], t[8] = from_right(w[0]), from_right(w[1]), from_right(t[0])
        for a in range(GROUPS):
            if a + 2 not in w:
                make(a + 2)
            s2 = at(a, -2) + at(a, 2)
            across = (t[a - 1] + t[a + 1]) + (w[a - 2] + w[a + 2])
            along = tall(coef[2, a], size) * s2 + tall(coef[1, a], size) * s1[a]
            along = along + tall(coef[0, a], size) * w[a]
            old = dst[a, pl.ds(r0, size), :]
            dst[a, pl.ds(r0, size), :] = along - (RATIO / ROOT) * across - old

    def axle(self, ax, loads, number, step, i):
        base = (number * self.steps + step) * LANES + i
        row, group, spot, kind = (ax[base + field * self.axles] for field in range(4))
        return row, group, spot, loads[kind]

    def sweep(self, cur, prev, coef, ax, loads, number, wanted, tile_index, grade):
        origin = tile_index * self.tile - REACH

        def advance_once(src, dst, step, around, scale):
            lane = lane_index(1)
            for i in range(self.axles):
                row, group, spot, weight = self.axle(ax, loads, number, step, i)
                local = row - origin
                inside = jnp.logical_and(local >= 0, local < self.rows)
                force = jnp.where(inside, weight * (-RATIO * scale), 0.0)
                place = jnp.where(inside, local, 0) + MARGIN
                here = dst[group, pl.ds(place, 1), :]
                dst[group, pl.ds(place, 1), :] = here + jnp.where(lane == spot, force, 0.0)
            first, last = MARGIN + REACH - around, MARGIN + REACH + self.tile + around
            while first < last:
                size = min(32, last - first)
                self.block(src, dst, coef, first, size)
                first += size
            self.clear_outside(dst, tile_index)

        for first in range(0, self.steps, 4):
            around = wanted + 2 * (self.steps - first)

            def two(half, scale):
                advance_once(cur, prev, 2 * half, around, scale)
                advance_once(prev, cur, 2 * half + 1, around, scale * (1.0 / ROOT))
                return scale * (1.0 / DECAY)

            start = jnp.float32(grade * DECAY ** (-0.5 * (first + 1)))
            lax.fori_loop(first // 2, first // 2 + 2, two, start)

    def state_copies(self, state, cur, prev, sems, out):
        place = pl.ds(MARGIN + REACH - KEPT, self.tile + 2 * KEPT)
        copies = []
        for f, ref in enumerate((cur, prev)):
            ends = (ref.at[:, place, :], state.at[f])
            copies.append(pltpu.make_async_copy(*(ends if out else ends[::-1]), sems.at[f]))
        return copies

    def inside(self, tile_index):
        row = lax.broadcasted_iota(jnp.int32, (self.crows, LANES), 0)
        row = row + (tile_index * (self.tile // 4) - CREACH)
        return jnp.logical_and(row >= 0, row < self.span * (self.tile // 4))

    def restricted(self, cur, prev, tile_index, grade):
        keep = self.inside(tile_index)
        fields = []
        for ref, scale in ((cur, 0.0625 / grade), (prev, 0.0625 / (grade * ROOT))):
            halves = []
            for g in range(2):
                total = None
                for a in range(4 * g, 4 * g + 4):
                    for j in range(4):
                        piece = ref[a, pl.ds(MARGIN + j, self.crows, stride=4), :]
                        total = piece if total is None else total + piece
                halves.append(jnp.where(keep, total * scale, 0.0))
            fields.append(halves)
        now, before = fields
        return now, [now[g] - before[g] for g in range(2)]

    def add_prolonged(self, cur, prev, field, fresh, grade, cut=0):
        count = self.crows - 2 * cut
        now = [value[cut : cut + count] for value in field[0]]
        change = [value[cut : cut + count] for value in field[1]]
        for g in range(2):
            before = (now[g] - change[g]) * (grade * ROOT)
            after = now[g] * grade
            for a in range(4 * g, 4 * g + 4):
                for j in range(4):
                    place = pl.ds(MARGIN + 4 * cut + j, count, stride=4)
                    if fresh:
                        cur[a, place, :] = after
                        prev[a, place, :] = before
                    else:
                        cur[a, place, :] = cur[a, place, :] + after
                        prev[a, place, :] = prev[a, place, :] + before

    def coarse_loads(self, cload, ax, loads, number, tile_index):
        origin = tile_index * (self.tile // 4) - CREACH
        lane = lane_index(1)
        scale = TIME_STEP * self.coarse_tau / (16.0 * self.steps)

        for step in range(self.steps):
            for i in range(self.axles):
                row, group, spot, weight = self.axle(ax, loads, number, step, i)
                local = (row >> 2) - origin
                inside = jnp.logical_and(local >= 0, local < self.crows)
                force = jnp.where(inside, scale * weight, 0.0)
                place = jnp.where(inside, local, 0) + MARGIN
                group = group >> 2
                here = cload[group, pl.ds(place, 1), :]
                cload[group, pl.ds(place, 1), :] = here + jnp.where(lane == spot, force, 0.0)

    def coarse(self, field, cwork, ccoef, tile_index, cload=None):
        now, change = field
        rows = self.crows
        for g in range(2):
            cwork[g, pl.ds(MARGIN, rows), :] = now[g]

        def at(g, offset):
            return cwork[g, pl.ds(MARGIN + offset, rows), :]

        keep = self.inside(tile_index)
        w = now
        s1 = [at(g, -1) + at(g, 1) for g in range(2)]
        s2 = [at(g, -2) + at(g, 2) for g in range(2)]
        t = [s1[g] - 6.0 * w[g] for g in range(2)]
        left, right = [from_left(t[1]), t[0]], [t[1], from_right(t[0])]
        kappa = TIME_STEP * self.coarse_tau / COARSE_SPACING
        grown, moved = [], []
        for g in range(2):
            s = tall(ccoef[g], rows)
            across = (left[g] + right[g]) + (from_left(w[g]) + from_right(w[g]))
            stiff = across + s * s2[g] - (4.0 * s + 2.0) * s1[g] + (6.0 * s + 10.0) * w[g]
            value = (1.0 - self.coarse_tau * DAMPING) * change[g] - kappa * stiff
            if cload is not None:
                value = value + cload[g, pl.ds(MARGIN, rows), :]
            value = jnp.where(keep, value, 0.0)
            moved.append(value)
            grown.append(w[g] + (self.coarse_tau / TIME_STEP) * value)
        return grown, moved


def put(ref, slot, field):
    for f in range(2):
        for g in range(2):
            ref[slot, f, g] = field[f][g]


def get(ref, slot):
    return [[ref[slot, f, g] for g in range(2)] for f in range(2)]


def plus(x, y):
    return [[x[f][g] + y[f][g] for g in range(2)] for f in range(2)]


def minus(x, y):
    return [[x[f][g] - y[f][g] for g in range(2)] for f in range(2)]


def load_rows(ref, cur, prev, offset, count, beside=None):
    half = count // 2

    def one(j, carry):
        r = pl.multiple_of(j * half, 8)
        fields = []
        for f in range(2):
            fields.append(interleave(
                [ref[f, pl.ds(r, half), q * LANES : (q + 1) * LANES] for q in range(GROUPS)]))
        place = pl.multiple_of(offset + r, 8)
        for a in range(GROUPS):
            cur[a, pl.ds(place, half), :] = fields[0][a]
            prev[a, pl.ds(place, half), :] = ROOT * (fields[0][a] - TIME_STEP * fields[1][a])
        if beside is not None:
            beside(j)
        return carry

    lax.fori_loop(0, 2, one, 0)


def own_kernel(plan):
    def body(table, loads, classes, axle_rows, axle_cols, axle_class, start, own, coef, ccoef, packed,
             loads_out):
        packed[...] = jnp.zeros(packed.shape, jnp.int32)
        cols = axle_cols[...]
        spot = ((cols >> 3) & 15) * 8 + (cols >> 7)
        for field, value in enumerate((axle_rows[...], cols & 7, spot, axle_class[...])):
            packed[:, field * plan.axles : (field + 1) * plan.axles] = value
        for entry in range(loads.shape[0]):
            loads_out[entry] = loads[entry]
        plan.stiffness(classes, table, coef, ccoef)
        load_rows(start, own.at[0], own.at[1], 0, plan.tile)

    return body


def arrival_kernel(plan):
    def body(meta, ax, loads, mine, near, cload):
        cload[...] = jnp.zeros(cload.shape, jnp.float32)

        def beside(number):
            plan.coarse_loads(cload.at[number], ax, loads, number, meta[1])

        load_rows(mine, near.at[0], near.at[1], 0, REACH, beside)

    return body


def first_kernel(plan):
    def body(meta, ax, loads, coef, ccoef, own, near, other, cload, state, send, keep, cwork, cur, prev,
             sems):
        number, tile_index = meta[0], meta[1]
        for g in range(2):
            cwork[g] = jnp.zeros((plan.cbuf, LANES), jnp.float32)
        even = ((tile_index + number) & 1) == 0
        below = MARGIN + REACH + plan.tile
        near_first = pl.multiple_of(jnp.where(even, below, MARGIN), 8)
        for f, ref in enumerate((cur, prev)):
            for a in range(GROUPS):
                ref[a, pl.ds(0, MARGIN), :] = jnp.zeros((MARGIN, LANES), jnp.float32)
                ref[a, pl.ds(MARGIN + plan.rows, MARGIN), :] = jnp.zeros((MARGIN, LANES), jnp.float32)
                ref[a, pl.ds(MARGIN + REACH, plan.tile), :] = own[f, a]
                ref[a, pl.ds(near_first, REACH), :] = near[f, a]
        load_rows(other, cur, prev, jnp.where(even, MARGIN, below), REACH)
        plan.clear_outside(cur, tile_index)
        plan.clear_outside(prev, tile_index)
        send[...] = jnp.zeros(send.shape, jnp.float32)

        def sweep(slice_number, wanted, grade):
            plan.sweep(cur, prev, coef, ax, loads, slice_number, wanted, tile_index, grade)

        once, twice = plan.grown, plan.grown * plan.grown

        @pl.when(number >= 2)
        def _():
            put(keep, 0, plan.restricted(cur, prev, tile_index, 1.0))

        sweep(0, 32, 1.0)

        @pl.when(number >= 2)
        def _():
            chain = plan.coarse(get(keep, 0), cwork, ccoef, tile_index, cload.at[0])
            put(keep, 0, chain)
            gap = minus(plan.restricted(cur, prev, tile_index, once), chain)
            put(keep, 1, plan.coarse(gap, cwork, ccoef, tile_index))

        @pl.when(number == 3)
        def _():
            put(keep, 0, plan.coarse(get(keep, 0), cwork, ccoef, tile_index, cload.at[1]))

        @pl.when((number & 1) == 1)
        def _():
            sweep(1, 16, once)

        @pl.when(number == 3)
        def _():
            restricted = plan.restricted(cur, prev, tile_index, twice)
            put(send, 0, restricted)
            put(keep, 2, restricted)

        @pl.when(number == 3)
        def _():
            plan.add_prolonged(cur, prev, get(keep, 0), True, 1.0)
            sweep(2, 16, 1.0)
            put(keep, 3, plan.restricted(cur, prev, tile_index, once))

        @pl.when(number == 2)
        def _():
            plan.add_prolonged(cur, prev, get(keep, 0), True, 1.0)
            sweep(1, 24, 1.0)
            restricted = plan.restricted(cur, prev, tile_index, once)
            put(send, 0, restricted)
            correction = get(keep, 1)
            put(keep, 3, plus(restricted, correction))
            plan.add_prolonged(cur, prev, correction, False, once)
            sweep(2, 8, once)
            put(send, 1, plan.restricted(cur, prev, tile_index, twice))

        copies = plan.state_copies(state, cur, prev, sems, True)
        for copy in copies:
            copy.start()
        for copy in copies:
            copy.wait()

    return body


def second_kernel(plan):
    def body(meta, ax, loads, coef, ccoef, state, keep, got, out, cwork, cur, prev, corr, sems, ready):
        number, tile_index = meta[0], meta[1]
        copies = plan.state_copies(state, cur, prev, sems, False)
        for copy in copies:
            copy.start()
        for g in range(2):
            cwork[g] = jnp.zeros((plan.cbuf, LANES), jnp.float32)
        @pl.when(number == 2)
        def _():
            gap = minus(get(got, 0), get(keep, 3))
            put(corr, 0, plan.coarse(gap, cwork, ccoef, tile_index))

        @pl.when(number == 3)
        def _():
            second = plus(get(got, 0), get(keep, 1))
            third = plan.coarse(minus(second, get(keep, 0)), cwork, ccoef, tile_index)
            put(corr, 1, third)
            early = plan.coarse(minus(get(keep, 2), second), cwork, ccoef, tile_index)
            gap = minus(plus(early, get(got, 1)), plus(get(keep, 3), third))
            put(corr, 0, plan.coarse(gap, cwork, ccoef, tile_index))

        for copy in copies:
            copy.wait()

        @pl.when(number == 3)
        def _():
            plan.add_prolonged(cur, prev, get(corr, 1), False, plan.grown, 8)
            plan.sweep(cur, prev, coef, ax, loads, 3, 0, tile_index, plan.grown)

        @pl.when(number >= 2)
        def _():
            plan.add_prolonged(cur, prev, get(corr, 0), False, plan.grown * plan.grown, 8)

        back = jnp.where(number == 0, 1.0 / plan.grown, 1.0 / (plan.grown * plan.grown))
        parts = []
        size = plan.tile // 2
        for j in range(2):
            rows = pl.ds(j * size, size)
            place = pl.ds(MARGIN + REACH + j * size, size)
            now = [cur[a, place, :] * back for a in range(GROUPS)]
            speed = [(now[a] - prev[a, place, :] * (back * (1.0 / ROOT))) * (1.0 / TIME_STEP) for a in range(GROUPS)]
            for f, pieces in enumerate((interleave(now), interleave(speed))):
                for q in range(GROUPS):
                    ready[f, rows, q * LANES : (q + 1) * LANES] = pieces[q]
            parts.append(pltpu.make_async_copy(ready.at[:, rows, :], out.at[0, :, rows, :], sems.at[2 + j]))
            parts[j].start()
        for part in parts:
            part.wait()

    return body


def paired_plan(mesh):
    slices, tiles = mesh.shape["tm"], mesh.shape["span"]

    def joint(slice_number, tile_index):
        return slice_number * tiles + tile_index

    halos = []
    for k in range(slices):
        for s in range(tiles):
            partner = s + 1 if (s + k) % 2 == 0 else s - 1
            target = joint(k, partner) if 0 <= partner < tiles else joint(k ^ 2, s)
            halos.append((joint(k, s), target))
    swap = [(k, k ^ 1) for k in range(slices)]
    smem = pl.BlockSpec(memory_space=pltpu.SMEM)
    vmem = pl.BlockSpec(memory_space=pltpu.VMEM)
    hbm = pl.BlockSpec(memory_space=pl.ANY)
    params = pltpu.CompilerParams(vmem_limit_bytes=40 * 2**20)

    def on_pair(start_state, stiff_class, class_stiffness, axle_rows, axle_cols, axle_class, load_table):
        tile_rows = start_state.shape[1]
        steps, axles = axle_rows.shape
        plan = Plan(tile_rows, tiles, steps, axles)
        number = lax.axis_index("tm")
        tile_index = lax.axis_index("span")
        even = ((tile_index + number) & 1) == 0
        edge = lax.dynamic_slice_in_dim(
            start_state, jnp.where(even, tile_rows - REACH, 0), REACH, axis=1)
        mine = lax.ppermute(edge, ("tm", "span"), halos)
        f32 = jnp.float32
        classes = stiff_class.reshape(1, -1)

        def shape(*dims):
            return jax.ShapeDtypeStruct(dims, f32)

        own, coef, ccoef, packed, loads = pl.pallas_call(
            own_kernel(plan),
            out_shape=(
                shape(2, GROUPS, tile_rows, LANES),
                shape(3, GROUPS, 8, LANES),
                shape(2, 8, LANES),
                jax.ShapeDtypeStruct((steps, LANES), jnp.int32),
                shape(*load_table.shape),
            ),
            in_specs=[smem, smem] + [vmem] * 5,
            out_specs=(vmem, vmem, vmem, vmem, smem),
            compiler_params=params,
        )(class_stiffness, load_table, classes, axle_rows, axle_cols, axle_class, start_state)
        ax = lax.all_gather(packed, "tm").reshape(-1)
        mine, ax = lax.optimization_barrier((mine, ax))
        other = lax.ppermute(mine, "tm", swap)
        meta = jnp.stack([number, tile_index]).astype(jnp.int32)
        coarse = (2, 2, plan.crows, LANES)
        frame = [
            pltpu.VMEM((2, plan.cbuf, LANES), f32),
            pltpu.VMEM((GROUPS, plan.buf, LANES), f32),
            pltpu.VMEM((GROUPS, plan.buf, LANES), f32),
        ]

        near, cload = pl.pallas_call(
            arrival_kernel(plan),
            out_shape=(shape(2, GROUPS, REACH, LANES), shape(2, 2, plan.cbuf, LANES)),
            in_specs=[smem, smem, smem, vmem],
            out_specs=(vmem, vmem),
            compiler_params=params,
        )(meta, ax, loads, mine)
        state, send, keep = pl.pallas_call(
            first_kernel(plan),
            out_shape=(shape(2, GROUPS, tile_rows + 2 * KEPT, LANES), shape(2, *coarse), shape(4, *coarse)),
            in_specs=[smem] * 3 + [vmem] * 6,
            out_specs=(hbm, vmem, vmem),
            scratch_shapes=frame + [pltpu.SemaphoreType.DMA((2,))],
            compiler_params=params,
        )(meta, ax, loads, coef, ccoef, own, near, other, cload)
        got = lax.ppermute(send, "tm", swap)
        return pl.pallas_call(
            second_kernel(plan),
            out_shape=shape(1, *start_state.shape),
            in_specs=[smem] * 3 + [vmem, vmem, hbm, vmem, vmem],
            out_specs=hbm,
            scratch_shapes=frame
            + [pltpu.VMEM((2,) + coarse, f32), pltpu.SemaphoreType.DMA((4,))]
            + [pltpu.VMEM(start_state.shape, f32)],
            compiler_params=params,
        )(meta, ax, loads, coef, ccoef, state, keep, got)

    return on_pair


def solution(mesh):
    in_specs = (
        P(None, ("parts", "span"), None),
        P("parts"),
        P(),
        P(("parts", "tm"), None),
        P(("parts", "tm"), None),
        P(("parts", "tm"), None),
        P(),
    )
    out_specs = P("tm", None, ("parts", "span"), None)
    body = paired_plan(mesh) if mesh.shape["tm"] == SLICES else on_device
    return jax.shard_map(body, mesh=mesh, in_specs=in_specs, out_specs=out_specs, check_vma=False)
```
